32 devices in a mesh: lat: 2 (over x), lon: 4 (over z), mp: 4 (over y, core).
Axes of the slice: x: 2, y: 2, z: 4, core: 2. Of those that a mesh axis runs over, the one named last changes fastest.
Arguments:
- sharp_resolution_vectors: bfloat16 [2, 32, 64, 512], P(None, 'lat', 'lon'), may hold values from -6 to 6
- queries_keys_weights: bfloat16 [512, 2, 512], P(None, None, 'mp'), may hold values from -0.03125 to 0.03125
- values_weights: bfloat16 [512, 512], P(None, 'mp'), may hold values from -0.25 to 0.25
- attn_result_weights: bfloat16 [512, 512], P('mp'), may hold values from -0.75 to 0.75
- score_factors_by_lane: float32 [8], replicated, may hold values from 1 to 8
- tile_merging_weights: bfloat16 [2048, 1024], P('lon', 'mp'), may hold values from -0.125 to 0.125
- shrunk_dense_first: bfloat16 [1024, 4096], P('lon', 'mp'), may hold values from -0.1875 to 0.1875
- shrunk_dense_second: bfloat16 [4096, 1024], P('mp', 'lon'), may hold values from -0.09375 to 0.09375
- tile_unfolding_weights: bfloat16 [1024, 2048], P('lon', 'mp'), may hold values from -0.1875 to 0.1875
- result_gradient: bfloat16 [2, 32, 64, 512], P(None, 'lat', ('lon', 'mp')), may hold values from -6 to 6
Outputs:
- output: bfloat16 [2, 32, 64, 512], P(None, 'lat', ('lon', 'mp'))
- fine_grad: bfloat16 [2, 32, 64, 512], P(None, 'lat', ('lon', 'mp'))
The draws below stay inside these ranges and needn't reach their ends.
All inputs are finite; a program needn't handle non-finite values.
Results may differ from the reference program's by a relative error of at most 0.02.
Values may be sent and summed in bfloat16 or wider, within the bound.
A program may use at most 128 MiB of HBM per device.

```python
import math
import jax
import jax.numpy as jnp
from jax import lax

MODEL_BREADTH = 512
SHARP_ATTN_LANES = 8
HID = 4096
TILE_SIDE_CELLS = 8
LEVELS = 2
HEAD = 64
NLAT = 32
NLON = 64


def shard_levels(key, extent, shards, smallest, top_value):
    gain = 1.0
    for dim, blocks in shards:
        steps = jax.random.uniform(jax.random.fold_in(jax.random.fold_in(key, 6), dim), (blocks,), jnp.float32, smallest / len(shards), top_value / len(shards))
        gain = gain * jnp.repeat(jnp.exp(steps), extent[dim] // blocks).reshape((-1,) + (1,) * (len(extent) - 1 - dim))
    return gain


def bell_draw(stream_key, shape, deviation, limit, shards=(), held_as=jnp.bfloat16):
    result = jax.random.normal(stream_key, shape, jnp.float32) * deviation
    if len(shards) > 0:
        result = shard_levels(stream_key, shape, shards, -0.22, 0.18) * result
    return jnp.clip(result, min=-limit, max=limit).astype(held_as)


def setup_inputs(seed: int = 0) -> dict:
    key_of = jax.random.split(jax.random.key(seed), 11)
    return {
        "sharp_resolution_vectors": bell_draw(key_of[0], (LEVELS, NLAT, NLON, MODEL_BREADTH), 1.0, 6.0, ((1, 2), (2, 4))),
        "queries_keys_weights": bell_draw(key_of[1], (MODEL_BREADTH, 2, MODEL_BREADTH), (HEAD * MODEL_BREADTH) ** -0.5, 0.03125, ((2, 4),)),
        "values_weights": bell_draw(key_of[2], (MODEL_BREADTH, MODEL_BREADTH), MODEL_BREADTH ** -0.5, 0.25, ((1, 4),)),
        "attn_result_weights": bell_draw(key_of[3], (MODEL_BREADTH, MODEL_BREADTH), HEAD ** -0.5, 0.75, ((0, 4),)),
        "score_factors_by_lane": jnp.clip(jnp.exp(jax.random.uniform(key_of[4], (SHARP_ATTN_LANES,), jnp.float32, math.log(1.0), math.log(8.0))), 1.0, 8.0),
        "tile_merging_weights": bell_draw(key_of[5], (4 * MODEL_BREADTH, 2 * MODEL_BREADTH), (4 * MODEL_BREADTH) ** -0.5, 0.125, ((0, 4), (1, 4))),
        "shrunk_dense_first": bell_draw(key_of[6], (2 * MODEL_BREADTH, HID), (2 * MODEL_BREADTH) ** -0.5, 0.1875, ((0, 4), (1, 4))),
        "shrunk_dense_second": bell_draw(key_of[7], (HID, 2 * MODEL_BREADTH), HID ** -0.5, 0.09375, ((0, 4), (1, 4))),
        "tile_unfolding_weights": bell_draw(key_of[8], (2 * MODEL_BREADTH, 4 * MODEL_BREADTH), (2 * MODEL_BREADTH) ** -0.5, 0.1875, ((0, 4), (1, 4))),
        "result_gradient": bell_draw(key_of[9], (LEVELS, NLAT, NLON, MODEL_BREADTH), 1.0, 6.0, ((1, 2), (2, 16))),
    }


epsilon = 1e-05

def layer_norm(inputs):
    values = inputs.astype(jnp.float32)
    center = values - lax.optimization_barrier(jnp.mean(values, -1, keepdims=True))
    spread = lax.optimization_barrier(jnp.mean(center * center, -1, keepdims=True))
    return center * lax.rsqrt(spread + epsilon)

def norm_round(inputs):
    return layer_norm(inputs).astype(jnp.bfloat16)

def activate(inputs):
    return jax.nn.gelu(inputs.astype(jnp.float32)).astype(jnp.bfloat16)

def unit_rows(tensor):
    values = tensor.astype(jnp.float32)
    length = jnp.sqrt(lax.optimization_barrier(jnp.sum(values * values, -1, keepdims=True)))
    return (values / jnp.maximum(length, 1.0)).astype(jnp.bfloat16)

def window_attention(query_rows, key_rows, value_rows, scales, allowed):
    query_unit = lax.optimization_barrier(unit_rows(query_rows)).astype(jnp.float32)
    key_unit = lax.optimization_barrier(unit_rows(key_rows)).astype(jnp.float32)
    scores = scales[None, :, None, None] * jnp.einsum('bthe,bshe->bhts', query_unit, key_unit, precision=lax.Precision.HIGHEST)
    weights_raw = jnp.where(allowed[:, None], jnp.exp(scores), 0.0)
    weights = lax.optimization_barrier((weights_raw / lax.optimization_barrier(jnp.sum(weights_raw, -1, keepdims=True))).astype(jnp.bfloat16))
    weighted_sum_vectors = jnp.einsum('bhts,bshe->bthe', weights.astype(jnp.float32), value_rows.astype(jnp.float32), precision=lax.Precision.HIGHEST)
    return weighted_sum_vectors.astype(jnp.bfloat16)

def to_windows(tensor):
    levels, row_count, column_count, depth = tensor.shape
    tensor = tensor.reshape(levels, row_count // TILE_SIDE_CELLS, TILE_SIDE_CELLS, column_count // TILE_SIDE_CELLS, TILE_SIDE_CELLS, depth).transpose(1, 3, 0, 2, 4, 5)
    return tensor.reshape(row_count // TILE_SIDE_CELLS, column_count // TILE_SIDE_CELLS, levels * TILE_SIDE_CELLS * TILE_SIDE_CELLS, depth)

def from_windows(tensor, levels):
    row_blocks, column_blocks, window_size, depth = tensor.shape
    tensor = tensor.reshape(row_blocks, column_blocks, levels, TILE_SIDE_CELLS, TILE_SIDE_CELLS, depth).transpose(2, 0, 3, 1, 4, 5)
    return tensor.reshape(levels, row_blocks * TILE_SIDE_CELLS, column_blocks * TILE_SIDE_CELLS, depth)

def tile_normalized_averager(stacked, scales, shifted_zone_marks):
    levels = stacked.shape[0]
    heads = scales.shape[0]
    width = stacked.shape[3] // 3
    windows = to_windows(stacked)
    row_blocks, column_blocks, window_size = windows.shape[:3]
    window_count = row_blocks * column_blocks

    def select_part(part_index):
        return windows[..., part_index * width:(part_index + 1) * width].reshape(window_count, window_size, heads, width // heads)
    token_label = jnp.broadcast_to(shifted_zone_marks.reshape(row_blocks, 1, TILE_SIDE_CELLS, 1), (row_blocks, levels, TILE_SIDE_CELLS, TILE_SIDE_CELLS)).reshape(row_blocks, window_size)
    allowed = token_label[:, :, None] == token_label[:, None, :]
    allowed = jnp.broadcast_to(allowed[:, None], (row_blocks, column_blocks, window_size, window_size)).reshape(window_count, window_size, window_size)
    weighted_sum_vectors = window_attention(select_part(0), select_part(1), select_part(2), scales, allowed)
    return from_windows(weighted_sum_vectors.reshape(row_blocks, column_blocks, window_size, width), levels)

def combined_normalizer(latent_finer_state):
    levels, row_count, column_count, width = latent_finer_state.shape
    grouped = latent_finer_state.reshape(levels, row_count // 2, 2, column_count // 2, 2, width).transpose(0, 1, 3, 2, 4, 5)
    grouped = grouped.reshape(levels, row_count // 2, column_count // 2, 4 * width)
    return layer_norm(grouped).astype(jnp.bfloat16)

def hourglass_single_pass(sharp_resolution_vectors, queries_keys_weights, values_weights, attn_result_weights, score_factors_by_lane, tile_merging_weights, shrunk_dense_first, shrunk_dense_second, tile_unfolding_weights):
    half_win = TILE_SIDE_CELLS // 2
    joined = jnp.concatenate([queries_keys_weights.reshape(MODEL_BREADTH, 2 * MODEL_BREADTH), values_weights], 1)
    rolled = jnp.roll(sharp_resolution_vectors, (-half_win, -half_win), axis=(1, 2))
    stacked = jnp.dot(norm_round(rolled), joined, preferred_element_type=jnp.float32).astype(jnp.bfloat16)
    position = jnp.arange(NLAT, dtype=jnp.int32)
    shifted_zone_marks = (position >= NLAT - TILE_SIDE_CELLS).astype(jnp.int32) + (position >= NLAT - half_win).astype(jnp.int32)
    attentive_sequence_blocks = NLAT // TILE_SIDE_CELLS
    north_south_slices = stacked.reshape(LEVELS, attentive_sequence_blocks, TILE_SIDE_CELLS, NLON, 3 * MODEL_BREADTH).transpose(1, 0, 2, 3, 4)
    weighted_sum_vectors = lax.map(lambda learned_weights_set: tile_normalized_averager(learned_weights_set[0], score_factors_by_lane, learned_weights_set[1]), (north_south_slices, shifted_zone_marks.reshape(attentive_sequence_blocks, TILE_SIDE_CELLS)))
    weighted_sum_vectors = weighted_sum_vectors.transpose(1, 0, 2, 3, 4).reshape(LEVELS, NLAT, NLON, MODEL_BREADTH)
    mixed_back = jnp.roll(weighted_sum_vectors, (half_win, half_win), axis=(1, 2))
    latent_finer_state = (sharp_resolution_vectors.astype(jnp.float32) + jnp.dot(mixed_back, attn_result_weights, preferred_element_type=jnp.float32)).astype(jnp.bfloat16)
    reduced_level = jnp.dot(combined_normalizer(latent_finer_state), tile_merging_weights, preferred_element_type=jnp.float32).astype(jnp.bfloat16)
    inner = jnp.dot(norm_round(reduced_level), shrunk_dense_first, preferred_element_type=jnp.float32).astype(jnp.bfloat16)
    coarse_out = (reduced_level.astype(jnp.float32) + jnp.dot(activate(inner), shrunk_dense_second, preferred_element_type=jnp.float32)).astype(jnp.bfloat16)
    expanded = jnp.dot(coarse_out, tile_unfolding_weights, preferred_element_type=jnp.float32).astype(jnp.bfloat16)
    expanded = expanded.reshape(LEVELS, NLAT // 2, NLON // 2, 2, 2, MODEL_BREADTH).transpose(0, 1, 3, 2, 4, 5).reshape(LEVELS, NLAT, NLON, MODEL_BREADTH)
    return (latent_finer_state.astype(jnp.float32) + expanded.astype(jnp.float32)).astype(jnp.bfloat16)

def reference(sharp_resolution_vectors, queries_keys_weights, values_weights, attn_result_weights, score_factors_by_lane, tile_merging_weights, shrunk_dense_first, shrunk_dense_second, tile_unfolding_weights, result_gradient):

    def forward(received_vectors):
        return hourglass_single_pass(received_vectors, queries_keys_weights, values_weights, attn_result_weights, score_factors_by_lane, tile_merging_weights, shrunk_dense_first, shrunk_dense_second, tile_unfolding_weights)
    output, pull_back = jax.vjp(forward, sharp_resolution_vectors)
    fine_grad = pull_back(result_gradient)[0]
    return (output, fine_grad)
```

```python
import jax
import jax.numpy as jnp
from jax import lax
from jax.sharding import PartitionSpec as P

TILE_SIDE_CELLS = 8


epsilon = 1e-05


def shifted(value, axis, by):
    devices = lax.axis_size(axis)
    return lax.ppermute(value, axis, [(i, (i + by) % devices) for i in range(devices)])


def layer_norm(inputs):
    values = inputs.astype(jnp.float32)
    center = values - jnp.mean(values, -1, keepdims=True)
    spread = jnp.mean(center * center, -1, keepdims=True)
    return center * lax.rsqrt(spread + epsilon)


def norm_round(inputs):
    return layer_norm(inputs).astype(jnp.bfloat16)


def activate(inputs):
    return jax.nn.gelu(inputs.astype(jnp.float32)).astype(jnp.bfloat16)


def unit_rows(tensor):
    values = tensor.astype(jnp.float32)
    length = jnp.sqrt(jnp.sum(values * values, -1, keepdims=True))
    return (values / jnp.maximum(length, 1.0)).astype(jnp.bfloat16)


def window_attention(query_rows, key_rows, value_rows, scales, allowed):
    query_unit = lax.optimization_barrier(unit_rows(query_rows)).astype(jnp.float32)
    key_unit = lax.optimization_barrier(unit_rows(key_rows)).astype(jnp.float32)
    scores = scales[None, :, None, None] * jnp.einsum(
        "bthe,bshe->bhts", query_unit, key_unit, precision=lax.Precision.HIGHEST
    )
    weights_raw = jnp.where(allowed[:, None], jnp.exp(scores), 0.0)
    weights = lax.optimization_barrier(
        (weights_raw / jnp.sum(weights_raw, -1, keepdims=True)).astype(jnp.bfloat16)
    )
    weighted_sum_vectors = jnp.einsum(
        "bhts,bshe->bthe",
        weights.astype(jnp.float32),
        value_rows.astype(jnp.float32),
        precision=lax.Precision.HIGHEST,
    )
    return weighted_sum_vectors.astype(jnp.bfloat16)


def to_windows(tensor):
    levels, row_count, column_count, depth = tensor.shape
    tensor = tensor.reshape(
        levels,
        row_count // TILE_SIDE_CELLS,
        TILE_SIDE_CELLS,
        column_count // TILE_SIDE_CELLS,
        TILE_SIDE_CELLS,
        depth,
    ).transpose(1, 3, 0, 2, 4, 5)
    return tensor.reshape(
        row_count // TILE_SIDE_CELLS,
        column_count // TILE_SIDE_CELLS,
        levels * TILE_SIDE_CELLS * TILE_SIDE_CELLS,
        depth,
    )


def from_windows(tensor, levels):
    row_blocks, column_blocks, window_size, depth = tensor.shape
    tensor = tensor.reshape(
        row_blocks, column_blocks, levels, TILE_SIDE_CELLS, TILE_SIDE_CELLS, depth
    ).transpose(2, 0, 3, 1, 4, 5)
    return tensor.reshape(
        levels, row_blocks * TILE_SIDE_CELLS, column_blocks * TILE_SIDE_CELLS, depth
    )


def tile_normalized_averager(stacked, scales, shifted_zone_marks):
    levels = stacked.shape[0]
    heads = scales.shape[0]
    width = stacked.shape[3] // 3
    windows = to_windows(stacked)
    row_blocks, column_blocks, window_size = windows.shape[:3]
    window_count = row_blocks * column_blocks

    def select_part(part_index):
        return windows[..., part_index * width : (part_index + 1) * width].reshape(
            window_count, window_size, heads, width // heads
        )

    token_label = jnp.broadcast_to(
        shifted_zone_marks.reshape(row_blocks, 1, TILE_SIDE_CELLS, 1),
        (row_blocks, levels, TILE_SIDE_CELLS, TILE_SIDE_CELLS),
    ).reshape(row_blocks, window_size)
    allowed = token_label[:, :, None] == token_label[:, None, :]
    allowed = jnp.broadcast_to(
        allowed[:, None], (row_blocks, column_blocks, window_size, window_size)
    ).reshape(window_count, window_size, window_size)
    weighted_sum_vectors = window_attention(
        select_part(0), select_part(1), select_part(2), scales, allowed
    )
    return from_windows(
        weighted_sum_vectors.reshape(row_blocks, column_blocks, window_size, width), levels
    )


def combined_normalizer(latent_finer_state):
    levels, row_count, column_count, width = latent_finer_state.shape
    grouped = latent_finer_state.reshape(
        levels, row_count // 2, 2, column_count // 2, 2, width
    ).transpose(0, 1, 3, 2, 4, 5)
    grouped = grouped.reshape(levels, row_count // 2, column_count // 2, 4 * width)
    return layer_norm(grouped).astype(jnp.bfloat16)


def roll_ahead(tensor):
    half_win = TILE_SIDE_CELLS // 2
    incoming = shifted(tensor[:, :half_win], "lat", -1)
    tensor = jnp.concatenate([tensor[:, half_win:], incoming], 1)
    incoming = shifted(tensor[:, :, :half_win], "lon", -1)
    return jnp.concatenate([tensor[:, :, half_win:], incoming], 2)


def roll_back(tensor):
    half_win = TILE_SIDE_CELLS // 2
    incoming = shifted(tensor[:, :, -half_win:], "lon", 1)
    tensor = jnp.concatenate([incoming, tensor[:, :, :-half_win]], 2)
    incoming = shifted(tensor[:, -half_win:], "lat", 1)
    return jnp.concatenate([incoming, tensor[:, :-half_win]], 1)


def gather_blocks(value, axis):
    devices = lax.axis_size(axis)
    pieces = [value] + [shifted(value, axis, by) for by in range(1, devices)]
    return pieces


def turn(value, blocks, by):
    rows, features = value.shape
    order = jnp.mod(by - jnp.arange(blocks), blocks)
    parts = value.reshape(rows, blocks, features // blocks)
    pieces = [lax.dynamic_index_in_dim(parts, order[k], 1, False) for k in range(blocks)]
    return jnp.concatenate(pieces, 1)


def sum_scatter(value, axis):
    moved = lax.all_to_all(value, axis, split_axis=0, concat_axis=0, tiled=True)
    return jnp.sum(moved.astype(jnp.float32), 0)


def sum_all(value, axis):
    devices = lax.axis_size(axis)
    rows, features = value.shape
    own = sum_scatter(value.reshape(devices, rows // devices, features), axis)
    return lax.all_gather(own.astype(value.dtype), axis, axis=0, tiled=True)


def per_device(
    sharp_resolution_vectors,
    queries_keys_weights,
    values_weights,
    attn_result_weights,
    score_factors_by_lane,
    tile_merging_weights,
    shrunk_dense_first,
    shrunk_dense_second,
    tile_unfolding_weights,
    result_gradient,
):
    levels, row_count, column_count, width = sharp_resolution_vectors.shape
    longitude_slice_size = lax.axis_size("mp")
    processor_position = lax.axis_index("mp")
    column_share = column_count // longitude_slice_size
    row_total = row_count * lax.axis_size("lat")
    position = lax.axis_index("lat") * row_count + jnp.arange(row_count, dtype=jnp.int32)
    shifted_zone_marks = (position >= row_total - TILE_SIDE_CELLS).astype(jnp.int32) + (
        position >= row_total - TILE_SIDE_CELLS // 2
    ).astype(jnp.int32)

    def columns_first(value):
        lev, rows, columns, feats = value.shape
        return jnp.moveaxis(
            value.reshape(lev, rows, longitude_slice_size, columns // longitude_slice_size, feats),
            2,
            0,
        )

    own_fine = lax.dynamic_slice_in_dim(
        sharp_resolution_vectors, processor_position * column_share, column_share, 2
    )
    local_width = values_weights.shape[1]
    features_on_processor = score_factors_by_lane.shape[0] // longitude_slice_size
    scale_share_local = lax.dynamic_slice_in_dim(
        score_factors_by_lane, processor_position * features_on_processor, features_on_processor, 0
    )
    joined = jnp.concatenate(
        [queries_keys_weights.reshape(width, 2 * local_width), values_weights], 1
    )
    source = roll_ahead(sharp_resolution_vectors)
    normed, norm_pull = jax.vjp(norm_round, source)
    stacked = jnp.dot(normed, joined, preferred_element_type=jnp.float32).astype(jnp.bfloat16)
    weighted_sum_vectors, attend_pull = jax.vjp(
        lambda packed: tile_normalized_averager(packed, scale_share_local, shifted_zone_marks),
        stacked,
    )
    mixed_back = roll_back(weighted_sum_vectors)
    partial_out = jnp.dot(mixed_back, attn_result_weights, preferred_element_type=jnp.float32)
    summed = sum_scatter(columns_first(partial_out.astype(jnp.bfloat16)), "mp")
    latent_finer_state = (own_fine.astype(jnp.float32) + summed).astype(jnp.bfloat16)
    merged_in, merge_pull = jax.vjp(combined_normalizer, latent_finer_state)
    gathered_in = lax.all_gather(merged_in, "mp", axis=2, tiled=True)
    coarse_in = turn(gathered_in.reshape(-1, 4 * width), lax.axis_size("lon"), lax.axis_index("lon"))
    coarse_count = coarse_in.shape[0]
    stripe_span = tile_merging_weights.shape[1]
    lon_count, lon_here = lax.axis_size("lon"), lax.axis_index("lon")
    merge_full = jnp.concatenate(gather_blocks(tile_merging_weights, "lon"), 0)
    inner_full = jnp.concatenate(gather_blocks(shrunk_dense_first, "lon"), 0)
    outer_full = jnp.concatenate(gather_blocks(shrunk_dense_second, "lon"), 1)
    expand_full = jnp.concatenate(gather_blocks(tile_unfolding_weights, "lon"), 0)
    merged_columns = jnp.dot(coarse_in, merge_full, preferred_element_type=jnp.float32)
    reduced_level = lax.all_gather(merged_columns.astype(jnp.bfloat16), "mp", axis=1, tiled=True)
    reduced_level = turn(reduced_level, lon_count, lon_here)
    coarse_norm, coarse_pull = jax.vjp(norm_round, reduced_level)
    inner = jnp.dot(coarse_norm, inner_full, preferred_element_type=jnp.float32)
    activated, activate_pull = jax.vjp(activate, inner.astype(jnp.bfloat16))
    outer = jnp.dot(activated, outer_full, preferred_element_type=jnp.float32)
    hidden_sum = sum_all(outer.astype(jnp.bfloat16), "mp").astype(jnp.float32)
    coarse_out = (reduced_level.astype(jnp.float32) + hidden_sum).astype(jnp.bfloat16)
    expanded = jnp.dot(coarse_out, expand_full, preferred_element_type=jnp.float32)
    expanded = expanded.astype(jnp.bfloat16).reshape(
        levels, row_count // 2, column_count // 2, 1, width
    )
    moved = lax.all_to_all(expanded, "mp", split_axis=2, concat_axis=3, tiled=True)
    fine_added = moved.reshape(levels, row_count // 2, column_share // 2, 2, 2, width).transpose(
        0, 1, 3, 2, 4, 5
    )
    fine_added = fine_added.reshape(levels, row_count, column_share, width)
    output = (latent_finer_state.astype(jnp.float32) + fine_added.astype(jnp.float32)).astype(
        jnp.bfloat16
    )
    delta_sub = result_gradient.reshape(
        levels, row_count // 2, 2, column_share // 2, 2, width
    ).transpose(0, 1, 3, 2, 4, 5)
    delta_sub = delta_sub.reshape(
        levels, row_count // 2, column_share // 2, longitude_slice_size, width
    )
    delta_expand = lax.all_to_all(delta_sub, "mp", split_axis=3, concat_axis=2, tiled=True).reshape(
        coarse_count, width
    )
    delta_out_part = jnp.dot(delta_expand, expand_full.T, preferred_element_type=jnp.float32)
    delta_coarse_out = sum_all(delta_out_part.astype(jnp.bfloat16), "mp")
    delta_active = jnp.dot(delta_coarse_out, outer_full.T, preferred_element_type=jnp.float32)
    delta_inner = activate_pull(delta_active.astype(jnp.bfloat16))[0]
    delta_norm_part = jnp.dot(delta_inner, inner_full.T, preferred_element_type=jnp.float32)
    delta_norm = sum_all(delta_norm_part.astype(jnp.bfloat16), "mp")
    delta_coarse = (
        delta_coarse_out.astype(jnp.float32) + coarse_pull(delta_norm)[0].astype(jnp.float32)
    ).astype(jnp.bfloat16)
    delta_columns = lax.dynamic_slice_in_dim(
        turn(delta_coarse, lon_count, lon_here), processor_position * stripe_span, stripe_span, 1
    )
    delta_merge_part = jnp.dot(delta_columns, merge_full.T, preferred_element_type=jnp.float32)
    delta_merge_part = turn(delta_merge_part.astype(jnp.bfloat16), lon_count, lon_here).reshape(
        levels, row_count // 2, column_count // 2, 4 * width
    )
    delta_merged = sum_scatter(columns_first(delta_merge_part), "mp").astype(jnp.bfloat16)
    delta_hidden_merge = merge_pull(delta_merged)[0]
    delta_hidden = (
        result_gradient.astype(jnp.float32) + delta_hidden_merge.astype(jnp.float32)
    ).astype(jnp.bfloat16)
    delta_mixed_back = jnp.dot(
        lax.all_gather(delta_hidden, "mp", axis=2, tiled=True),
        attn_result_weights.T,
        preferred_element_type=jnp.float32,
    ).astype(jnp.bfloat16)
    delta_mixed = roll_ahead(delta_mixed_back)
    delta_stacked = attend_pull(delta_mixed)[0]
    delta_normed_part = jnp.dot(delta_stacked, joined.T, preferred_element_type=jnp.float32)
    delta_normed = sum_all(
        delta_normed_part.astype(jnp.bfloat16).reshape(-1, width), "mp"
    ).reshape(delta_normed_part.shape)
    delta_source = norm_pull(delta_normed)[0]
    delta_source = roll_back(delta_source)
    own_delta = lax.dynamic_slice_in_dim(
        delta_source, processor_position * column_share, column_share, 2
    )
    fine_grad = (delta_hidden.astype(jnp.float32) + own_delta.astype(jnp.float32)).astype(
        jnp.bfloat16
    )
    return (output, fine_grad)


def solution(mesh):
    in_specs = (
        P(None, "lat", "lon", None),
        P(None, None, "mp"),
        P(None, "mp"),
        P("mp", None),
        P(),
        P("lon", "mp"),
        P("lon", "mp"),
        P("mp", "lon"),
        P("lon", "mp"),
        P(None, "lat", ("lon", "mp"), None),
    )
    out_specs = (P(None, "lat", ("lon", "mp"), None), P(None, "lat", ("lon", "mp"), None))
    return jax.shard_map(
        per_device, mesh=mesh, in_specs=in_specs, out_specs=out_specs, check_vma=False
    )
```

```python
import functools
import jax
import jax.numpy as jnp
from jax import lax
from jax.experimental import pallas as pl
from jax.experimental.pallas import tpu as pltpu
from jax.sharding import PartitionSpec as P

TILE_SIDE_CELLS = 8
HALF = TILE_SIDE_CELLS // 2

epsilon = 1e-05
bf16 = jnp.bfloat16
f32 = jnp.float32


def dot(a, b, ca=1, cb=0):
    return lax.dot_general(a, b, (((ca,), (cb,)), ((), ())), preferred_element_type=f32)


def norm_parts(values, axes):
    center = values - jnp.mean(values, axes, keepdims=True)
    spread = jnp.mean(center * center, axes, keepdims=True)
    scale = lax.rsqrt(spread + epsilon)
    return center * scale, scale


def norm_back(delta, normal, scale, axes):
    return scale * (
        delta
        - jnp.mean(delta, axes, keepdims=True)
        - normal * jnp.mean(delta * normal, axes, keepdims=True)
    )


GELU_A = 0.7978845608028654
GELU_B = 0.044715


def gelu(x):
    return 0.5 * x * (1.0 + jnp.tanh(GELU_A * (x + GELU_B * x * x * x)))


def gelu_back(x):
    t = jnp.tanh(GELU_A * (x + GELU_B * x * x * x))
    return 0.5 * (1.0 + t) + 0.5 * x * (1.0 - t * t) * GELU_A * (1.0 + 3.0 * GELU_B * x * x)


def unit(values):
    length = jnp.sqrt(jnp.sum(values * values, -1, keepdims=True))
    return values / jnp.maximum(length, 1.0)


def unit_back(delta, values):
    length = jnp.sqrt(jnp.sum(values * values, -1, keepdims=True))
    inverse = 1.0 / jnp.maximum(length, 1.0)
    share = jnp.where(length > 1.0, 1.0, jnp.where(length == 1.0, 0.5, 0.0))
    along = jnp.sum(delta * values, -1, keepdims=True)
    return delta * inverse - share * values * (along * inverse * inverse * inverse)


def kernel(
    sizes,
    x_ref,
    joined_ref,
    out_weight_ref,
    scale_ref,
    merge_ref,
    first_ref,
    second_ref,
    unfold_ref,
    g_ref,
    output_ref,
    grad_ref,
    xe,
    me,
    de,
    le,
    wm,
    wf,
    ws,
    wu,
    stacked_ref,
    probs_ref,
    attn_back,
    send_a,
    recv_a,
    merged_all,
    columns_all,
    send_o,
    recv_o,
    out_all,
    send_e,
    recv_e,
    delta_e,
    send_d,
    recv_d,
    delta_all,
    send_n,
    recv_n,
    send_c,
    columns_delta,
    send_m,
    recv_m,
    hidden_all,
    send_l,
    recv_l,
    send_sem,
    recv_sem,
    local_sem,
):
    n_lat, n_lon, n_mp, nbi, nbj, cells = sizes
    width = x_ref.shape[-1]
    la, lo, p = lax.axis_index("lat"), lax.axis_index("lon"), lax.axis_index("mp")
    rows_q = 4 * nbi * cells
    coarse_q = nbi * cells
    nwi, nwj = nbi // 2, nbj // 2
    window = 4 * 4 * cells
    split = 2 if n_lat == 2 else 1

    def plus(dlat, dlon, dmp):
        return {
            "lat": lax.rem(la + dlat + n_lat, n_lat),
            "lon": lax.rem(lo + dlon + n_lon, n_lon),
            "mp": lax.rem(p + dmp + n_mp, n_mp),
        }

    partners = set()
    for dlat, dlon in ((1, 0), (0, 1), (1, 1)):
        for sign in (1, -1):
            partners.add((sign * dlat % n_lat, sign * dlon % n_lon, 0))
    for by in range(1, n_lon):
        partners.add((0, by, 0))
    for by in range(1, n_mp):
        partners.add((0, 0, by))
    partners = sorted(partners)
    barrier = pltpu.get_barrier_semaphore()
    for offset in partners:
        pl.semaphore_signal(
            barrier, inc=1, device_id=plus(*offset), device_id_type=pl.DeviceIdType.MESH
        )
    pl.semaphore_wait(barrier, len(partners))

    count = [0]
    sent = []

    def send(src, dst, device):
        i = count[0]
        count[0] += 1
        copy = pltpu.make_async_remote_copy(
            src_ref=src,
            dst_ref=dst,
            send_sem=send_sem.at[i],
            recv_sem=recv_sem.at[i],
            device_id=device,
            device_id_type=pl.DeviceIdType.MESH,
        )
        copy.start()
        sent.append(copy)
        return copy

    def arrive(copies):
        for copy in copies:
            copy.wait_recv()

    def to_peers(src_of, dst):
        copies = []
        for by in range(1, n_mp):
            device = plus(0, 0, by)
            copies.append(send(src_of(device["mp"]), dst.at[p], device))
        return copies

    def sum_peers(own, dst):
        total = own.astype(f32)
        for by in range(1, n_mp):
            total = total + dst[lax.rem(p + by, n_mp)].astype(f32)
        return total

    halo = [
        send(x_ref.at[pl.ds(1, nbj - 1), :, 0], xe.at[pl.ds(1, nbj - 1), :, nbi], plus(-1, 0, 0)),
        send(x_ref.at[0, :, pl.ds(1, nbi - 1)], xe.at[nbj, :, pl.ds(1, nbi - 1)], plus(0, -1, 0)),
        send(x_ref.at[0, :, 0], xe.at[nbj, :, nbi], plus(-1, -1, 0)),
    ]
    gradient_moves = to_peers(lambda q: g_ref.at[q], delta_e)

    weights = ((merge_ref, wm), (first_ref, wf), (second_ref, ws), (unfold_ref, wu))
    own_copies = []
    weight_moves = []
    for i, (src, dst) in enumerate(weights):
        part = src.shape[0] // split
        mine = pl.ds(pl.multiple_of(la * part, part) if split > 1 else 0, part)
        copy = pltpu.make_async_copy(src, dst.at[lo], local_sem.at[i])
        copy.start()
        own_copies.append(copy)
        moves = []
        for by in range(1, n_lon):
            moves.append(send(src.at[mine], dst.at[lo, mine], plus(0, by, 0)))
        weight_moves.append((moves, mine))
    across = [None] * len(weights)

    def pass_on(i):
        dst = weights[i][1]
        moves, mine = weight_moves[i]
        across[i] = []
        for by in range(1, n_lon):
            moves[by - 1].wait_recv()
            if split > 1:
                owner = lax.rem(lo - by + n_lon, n_lon)
                across[i].append(send(dst.at[owner, mine], dst.at[owner, mine], plus(1, 0, 0)))

    def ready(i):
        arrive(across[i])
        own_copies[i].wait()

    xe[pl.ds(0, nbj), :, pl.ds(0, nbi)] = x_ref[...]
    arrive(halo)

    def window_blocks(ref):
        parts = []
        for wi in range(nwi):
            for wj in range(nwj):
                for u in range(2):
                    for v in range(2):
                        block = ref[2 * wj + v + 1, :, 2 * wi + u + 1].astype(f32)
                        parts.append(block.reshape(4 * cells, ref.shape[-1]))
        return jnp.concatenate(parts, 0)

    def block_at(index):
        rest, v = divmod(index, 2)
        rest, u = divmod(rest, 2)
        wi, wj = divmod(rest, nwj)
        return 2 * wj + v + 1, 2 * wi + u + 1

    source = window_blocks(xe)
    normed = norm_parts(source, -1)[0].astype(bf16)
    joined = joined_ref[...]
    stacked = dot(normed, joined).astype(bf16)
    stacked_ref[...] = stacked
    local = joined.shape[1] // 3
    heads = scale_ref.shape[0] // n_mp
    head = local // heads
    t_half = lax.broadcasted_iota(jnp.int32, (window, window), 0) // (window // 2)
    s_half = lax.broadcasted_iota(jnp.int32, (window, window), 1) // (window // 2)
    last = (la == n_lat - 1).astype(f32)
    same = (t_half == s_half).astype(f32)
    gate = jnp.maximum(same, 1.0 - last)

    def slices(w, h):
        def part(k):
            at = k * local + h * head
            return stacked_ref[pl.ds(w * window, window), at : at + head].astype(f32)

        return part(0), part(1), part(2)

    mixed_windows = []
    for w in range(nwi * nwj):
        per_head = []
        for h in range(heads):
            query, key, value = slices(w, h)
            scale = scale_ref[p * heads + h]
            scores = scale * dot(unit(query).astype(bf16), unit(key).astype(bf16), 1, 1)
            raw = jnp.exp(scores)
            if w // nwj == nwi - 1:
                raw = raw * gate
            prob = raw / jnp.sum(raw, -1, keepdims=True)
            probs_ref[w * heads + h] = prob
            per_head.append(dot(prob.astype(bf16), value.astype(bf16)))
        mixed_windows.append(jnp.concatenate(per_head, 1))
    mixed = jnp.concatenate(mixed_windows, 0)
    block_rows = 4 * cells
    for index in range(nbi * nbj):
        bj, bi = block_at(index)
        block = mixed[index * block_rows : (index + 1) * block_rows]
        me[bj, :, bi] = block.reshape(4, cells, local).astype(bf16)
    back = [
        send(me.at[pl.ds(1, nbj - 1), :, nbi], me.at[pl.ds(1, nbj - 1), :, 0], plus(1, 0, 0)),
        send(me.at[nbj, :, pl.ds(1, nbi - 1)], me.at[0, :, pl.ds(1, nbi - 1)], plus(0, 1, 0)),
        send(me.at[nbj, :, nbi], me.at[0, :, 0], plus(1, 1, 0)),
    ]
    pass_on(0)
    arrive(back)
    mixed_back = me[pl.ds(0, nbj), :, pl.ds(0, nbi)].astype(f32).reshape(n_mp * rows_q, local)
    partial = dot(mixed_back.astype(bf16), out_weight_ref[...]).astype(bf16)
    send_a[...] = partial.reshape(n_mp, rows_q, width)
    moves = to_peers(lambda q: send_a.at[q], recv_a)
    pass_on(1)
    arrive(moves)
    own_fine = x_ref[p].astype(f32).reshape(rows_q, width)
    hidden = (own_fine + sum_peers(send_a[p], recv_a)).astype(bf16)
    hidden = hidden.astype(f32).reshape(4, coarse_q, width)
    merge_normal, merge_scale = norm_parts(hidden, (0, 2))
    merged_all[p] = merge_normal.astype(bf16)
    moves = to_peers(lambda q: merged_all.at[p], merged_all)
    ready(0)
    merge_full = wm[...].reshape(4 * width, wm.shape[-1])
    arrive(moves)
    columns = jnp.zeros((n_mp * coarse_q, wm.shape[-1]), f32)
    for s in range(4):
        tokens = merged_all[:, s].reshape(n_mp * coarse_q, width)
        columns = columns + dot(tokens, merge_full[s * width : (s + 1) * width])
    columns_all[p] = columns.astype(bf16)
    moves = to_peers(lambda q: columns_all.at[p], columns_all)
    pass_on(2)
    pass_on(3)

    for q in range(n_mp):
        @pl.when(p == q)
        def _(q=q):
            delta_e[q] = g_ref[q]

    arrive(gradient_moves)
    ready(3)
    tokens_delta = delta_e[...].reshape(n_mp * coarse_q, width)
    unfold_full = wu[...].reshape(n_lon * wu.shape[1], width)
    coarse_width = unfold_full.shape[0]
    term = dot(tokens_delta, unfold_full, 1, 1).astype(bf16)
    send_d[...] = term.reshape(n_mp, coarse_q, coarse_width)
    moves_d = to_peers(lambda q: send_d.at[q], recv_d)

    arrive(moves)
    coarse = jnp.concatenate([columns_all[r] for r in range(n_mp)], 1).astype(f32)
    coarse_norm = norm_parts(coarse, -1)[0].astype(bf16)
    ready(1)
    first_full = wf[...].reshape(coarse_width, wf.shape[-1])
    inner = dot(coarse_norm, first_full).astype(bf16).astype(f32)
    activated = gelu(inner).astype(bf16)
    ready(2)
    outer = jnp.concatenate([dot(activated, ws[k]) for k in range(n_lon)], 1).astype(bf16)
    send_o[...] = outer.reshape(n_mp, coarse_q, coarse_width)
    moves_o = to_peers(lambda q: send_o.at[q], recv_o)

    arrive(moves_d)
    delta_own = sum_peers(send_d[p], recv_d).astype(bf16)
    delta_all[p] = delta_own
    moves_d = to_peers(lambda q: delta_all.at[p], delta_all)

    arrive(moves_o)
    own_coarse = jnp.concatenate(
        [columns_all[r, pl.ds(pl.multiple_of(p * coarse_q, coarse_q), coarse_q)] for r in range(n_mp)], 1
    ).astype(f32)
    out_all[p] = (own_coarse + sum_peers(send_o[p], recv_o)).astype(bf16)
    moves_o = to_peers(lambda q: out_all.at[p], out_all)

    arrive(moves_d)
    delta_coarse_out = delta_all[...].reshape(n_mp * coarse_q, coarse_width)
    second_width = ws.shape[-1]
    delta_active = jnp.zeros((n_mp * coarse_q, ws.shape[1]), f32)
    for k in range(n_lon):
        piece = delta_coarse_out[:, k * second_width : (k + 1) * second_width]
        delta_active = delta_active + dot(piece, ws[k], 1, 1)
    delta_inner = (delta_active.astype(bf16).astype(f32) * gelu_back(inner)).astype(bf16)
    term = dot(delta_inner, first_full, 1, 1).astype(bf16)
    send_n[...] = term.reshape(n_mp, coarse_q, coarse_width)
    moves_n = to_peers(lambda q: send_n.at[q], recv_n)

    arrive(moves_o)
    coarse_out = out_all[...].reshape(n_mp * coarse_q, coarse_width)
    send_e[...] = dot(coarse_out, unfold_full).astype(bf16).reshape(n_mp, coarse_q, width)
    moves_e = to_peers(lambda q: send_e.at[q], recv_e)

    arrive(moves_n)
    delta_norm = sum_peers(send_n[p], recv_n).astype(bf16).astype(f32)
    own_normal, own_scale = norm_parts(own_coarse, -1)
    pulled = norm_back(delta_norm, own_normal, own_scale, -1).astype(bf16).astype(f32)
    delta_coarse = (delta_own.astype(f32) + pulled).astype(bf16)
    stripe = wm.shape[-1]
    for r in range(n_mp):
        send_c[r] = delta_coarse[:, r * stripe : (r + 1) * stripe]
    moves_c = to_peers(lambda q: send_c.at[q], columns_delta)
    columns_delta[p] = send_c[p]

    arrive(moves_e)
    recv_e[p] = send_e[p]
    output_ref[...] = (hidden + recv_e[...].astype(f32)).astype(bf16)

    arrive(moves_c)
    delta_columns = columns_delta[...].reshape(n_mp * coarse_q, stripe)
    for s in range(4):
        piece = dot(delta_columns, merge_full[s * width : (s + 1) * width], 1, 1).astype(bf16)
        send_m[:, s] = piece.reshape(n_mp, coarse_q, width)
    moves = to_peers(lambda q: send_m.at[q], recv_m)
    arrive(moves)
    delta_merged = sum_peers(send_m[p], recv_m).astype(bf16).astype(f32)
    pulled = norm_back(delta_merged, merge_normal, merge_scale, (0, 2)).astype(bf16).astype(f32)
    delta_hidden = (g_ref[...].astype(f32) + pulled).astype(bf16)
    hidden_all[p] = delta_hidden
    moves = to_peers(lambda q: hidden_all.at[p], hidden_all)
    arrive(moves)

    delta_back = dot(
        hidden_all[...].reshape(n_mp * rows_q, width), out_weight_ref[...], 1, 1
    ).astype(bf16).astype(f32)
    de[pl.ds(0, nbj), :, pl.ds(0, nbi)] = delta_back.reshape(nbj, 4, nbi, cells, local).astype(bf16)
    halo = [
        send(de.at[pl.ds(1, nbj - 1), :, 0], de.at[pl.ds(1, nbj - 1), :, nbi], plus(-1, 0, 0)),
        send(de.at[0, :, pl.ds(1, nbi - 1)], de.at[nbj, :, pl.ds(1, nbi - 1)], plus(0, -1, 0)),
        send(de.at[0, :, 0], de.at[nbj, :, nbi], plus(-1, -1, 0)),
    ]
    arrive(halo)
    delta_mixed = window_blocks(de).astype(bf16)
    for w in range(nwi * nwj):
        grads = [[], [], []]
        for h in range(heads):
            query, key, value = slices(w, h)
            scale = scale_ref[p * heads + h]
            prob = probs_ref[w * heads + h]
            delta = delta_mixed[w * window : (w + 1) * window, h * head : (h + 1) * head]
            delta_prob = dot(delta, value.astype(bf16), 1, 1).astype(bf16).astype(f32)
            delta_value = dot(prob.astype(bf16), delta, 0, 0)
            inside = jnp.sum(delta_prob * prob, -1, keepdims=True)
            delta_score = (scale * (prob * (delta_prob - inside))).astype(bf16)
            delta_query = dot(delta_score, unit(key).astype(bf16)).astype(bf16).astype(f32)
            delta_key = dot(delta_score, unit(query).astype(bf16), 0, 0).astype(bf16).astype(f32)
            grads[0].append(unit_back(delta_query, query))
            grads[1].append(unit_back(delta_key, key))
            grads[2].append(delta_value)
        attn_back[pl.ds(w * window, window), :] = jnp.concatenate(
            grads[0] + grads[1] + grads[2], 1
        ).astype(bf16)
    delta_normed = dot(attn_back[...], joined_ref[...], 1, 1)
    for index in range(nbi * nbj):
        bj, bi = block_at(index)
        block = delta_normed[index * block_rows : (index + 1) * block_rows]
        send_l[bj % n_mp, :, bi - 1] = block.reshape(4, cells, width).astype(bf16)
    moves = to_peers(lambda q: send_l.at[q], recv_l)
    column = jnp.where(p == 0, n_mp, p)
    own_source = xe[column, :, pl.ds(1, nbi)].astype(f32)
    source_normal, source_scale = norm_parts(own_source, -1)
    arrive(moves)
    delta_source = sum_peers(send_l[p], recv_l).astype(bf16).astype(f32)
    delta_source = norm_back(delta_source, source_normal, source_scale, -1)
    le[:, pl.ds(1, nbi)] = delta_source.astype(bf16)

    final = count[0]
    count[0] += 2

    def last_copy(i, src, dst, device):
        return pltpu.make_async_remote_copy(
            src_ref=src,
            dst_ref=dst,
            send_sem=send_sem.at[final + i],
            recv_sem=recv_sem.at[final + i],
            device_id=device,
            device_id_type=pl.DeviceIdType.MESH,
        )

    first_column = (p == 0).astype(jnp.int32)
    corner = last_copy(0, le.at[:, nbi], le.at[:, 0], plus(1, first_column, 0))
    corner.start()
    rest = last_copy(1, le.at[:, pl.ds(1, nbi - 1)], recv_l.at[p, :, pl.ds(1, nbi - 1)], plus(0, 1, 0))

    @pl.when(p == 0)
    def _():
        rest.start()
        rest.wait()

    @pl.when(p != 0)
    def _():
        recv_l[p, :, pl.ds(1, nbi - 1)] = le[:, pl.ds(1, nbi - 1)]

    corner.wait()
    recv_l[p, :, 0] = le[:, 0]
    own_delta = recv_l[p].astype(f32).reshape(4, coarse_q, width)
    grad_ref[...] = (delta_hidden.astype(f32) + own_delta).astype(bf16)
    for copy in sent:
        copy.wait_send()


def per_device(
    sharp_resolution_vectors,
    queries_keys_weights,
    values_weights,
    attn_result_weights,
    score_factors_by_lane,
    tile_merging_weights,
    shrunk_dense_first,
    shrunk_dense_second,
    tile_unfolding_weights,
    result_gradient,
):
    levels, row_count, column_count, width = sharp_resolution_vectors.shape
    n_lat, n_lon, n_mp = (lax.axis_size(name) for name in ("lat", "lon", "mp"))
    nbi, nbj = row_count // HALF, column_count // HALF
    cells = levels * (HALF // 2) ** 2
    assert nbj == n_mp and tile_unfolding_weights.shape[1] == width

    def to_blocks(value):
        columns = value.shape[2] // HALF
        value = value.reshape(levels, nbi, HALF // 2, 2, columns, HALF // 2, 2, width)
        value = value.transpose(4, 3, 6, 1, 0, 2, 5, 7)
        return value.reshape(columns, 4, nbi, cells, width)

    def from_blocks(value):
        value = value.reshape(2, 2, nbi, levels, HALF // 2, HALF // 2, width)
        value = value.transpose(3, 2, 4, 0, 5, 1, 6)
        return value.reshape(levels, row_count, HALF, width)

    blocks = to_blocks(sharp_resolution_vectors)
    local = values_weights.shape[1]
    joined = jnp.concatenate([queries_keys_weights.reshape(width, 2 * local), values_weights], 1)
    coarse_q = nbi * cells
    rows_q = 4 * coarse_q
    gradient = to_blocks(result_gradient).reshape(4, coarse_q, width)
    weights = (tile_merging_weights, shrunk_dense_first, shrunk_dense_second, tile_unfolding_weights)
    coarse_width = n_lon * tile_unfolding_weights.shape[0]
    stripe = tile_merging_weights.shape[1]
    heads = score_factors_by_lane.shape[0] // n_mp
    window = 16 * cells
    windows = (nbi // 2) * (nbj // 2)
    vm = pltpu.VMEM
    fine = (n_mp, rows_q, width)
    coarse = (n_mp, coarse_q, coarse_width)
    quarter = (n_mp, coarse_q, width)
    grouped = (n_mp, 4, coarse_q, width)
    pieces = (n_mp, 4, nbi, cells, width)
    scratch = [
        vm((nbj + 1, 4, nbi + 1, cells, width), bf16),
        vm((nbj + 1, 4, nbi + 1, cells, local), bf16),
        vm((nbj + 1, 4, nbi + 1, cells, local), bf16),
        vm((4, nbi + 1, cells, width), bf16),
        *[vm((n_lon,) + w.shape, bf16) for w in weights],
        vm((windows * window, 3 * local), bf16),
        vm((windows * heads, window, window), f32),
        vm((windows * window, 3 * local), bf16),
        vm(fine, bf16),
        vm(fine, bf16),
        vm(grouped, bf16),
        vm((n_mp, n_mp * coarse_q, stripe), bf16),
        vm(coarse, bf16),
        vm(coarse, bf16),
        vm(coarse, bf16),
        vm(quarter, bf16),
        vm(quarter, bf16),
        vm(quarter, bf16),
        vm(coarse, bf16),
        vm(coarse, bf16),
        vm(coarse, bf16),
        vm(coarse, bf16),
        vm(coarse, bf16),
        vm((n_mp, coarse_q, stripe), bf16),
        vm((n_mp, coarse_q, stripe), bf16),
        vm(grouped, bf16),
        vm(grouped, bf16),
        vm(grouped, bf16),
        vm(pieces, bf16),
        vm(pieces, bf16),
    ]
    copies = 11 + 14 * (n_mp - 1) + 8 * (n_lon - 1)
    scratch += [
        pltpu.SemaphoreType.DMA((copies,)),
        pltpu.SemaphoreType.DMA((copies,)),
        pltpu.SemaphoreType.DMA((4,)),
    ]
    inside = pl.BlockSpec(memory_space=pltpu.VMEM)
    outside = pl.BlockSpec(memory_space=pl.ANY)
    shape = jax.ShapeDtypeStruct((4, coarse_q, width), bf16)
    output, grad = pl.pallas_call(
        functools.partial(kernel, (n_lat, n_lon, n_mp, nbi, nbj, cells)),
        out_shape=(shape, shape),
        in_specs=[inside] * 3
        + [pl.BlockSpec(memory_space=pltpu.SMEM)]
        + [outside] * 4
        + [inside],
        out_specs=(inside, inside),
        scratch_shapes=scratch,
        compiler_params=pltpu.CompilerParams(
            collective_id=0, has_side_effects=True, vmem_limit_bytes=56 * 2**20
        ),
        name="unet_step",
    )(blocks, joined, attn_result_weights, score_factors_by_lane, *weights, gradient)
    return (from_blocks(output), from_blocks(grad))


def solution(mesh):
    in_specs = (
        P(None, "lat", "lon", None),
        P(None, None, "mp"),
        P(None, "mp"),
        P("mp", None),
        P(),
        P("lon", "mp"),
        P("lon", "mp"),
        P("mp", "lon"),
        P("lon", "mp"),
        P(None, "lat", ("lon", "mp"), None),
    )
    out_specs = (P(None, "lat", ("lon", "mp"), None), P(None, "lat", ("lon", "mp"), None))
    return jax.shard_map(
        per_device, mesh=mesh, in_specs=in_specs, out_specs=out_specs, check_vma=False
    )
```

```python
import functools
import jax
import jax.numpy as jnp
from jax import lax
from jax.experimental import pallas as pl
from jax.experimental.pallas import tpu as pltpu
from jax.sharding import PartitionSpec as P

TILE_SIDE_CELLS = 8
HALF = TILE_SIDE_CELLS // 2

epsilon = 1e-05
bf16 = jnp.bfloat16
f32 = jnp.float32


def dot(a, b, ca=1, cb=0):
    return lax.dot_general(a, b, (((ca,), (cb,)), ((), ())), preferred_element_type=f32)


def norm_parts(values, axes):
    center = values - jnp.mean(values, axes, keepdims=True)
    spread = jnp.mean(center * center, axes, keepdims=True)
    scale = lax.rsqrt(spread + epsilon)
    return center * scale, scale


def norm_back(delta, normal, scale, axes):
    return scale * (
        delta
        - jnp.mean(delta, axes, keepdims=True)
        - normal * jnp.mean(delta * normal, axes, keepdims=True)
    )


GELU_A = 0.7978845608028654
GELU_B = 0.044715


def gelu(x):
    return 0.5 * x * (1.0 + jnp.tanh(GELU_A * (x + GELU_B * x * x * x)))


def gelu_back(x):
    t = jnp.tanh(GELU_A * (x + GELU_B * x * x * x))
    return 0.5 * (1.0 + t) + 0.5 * x * (1.0 - t * t) * GELU_A * (1.0 + 3.0 * GELU_B * x * x)


def unit(values):
    length = jnp.sqrt(jnp.sum(values * values, -1, keepdims=True))
    return values / jnp.maximum(length, 1.0)


def unit_back(delta, values):
    length = jnp.sqrt(jnp.sum(values * values, -1, keepdims=True))
    inverse = 1.0 / jnp.maximum(length, 1.0)
    share = jnp.where(length > 1.0, 1.0, jnp.where(length == 1.0, 0.5, 0.0))
    along = jnp.sum(delta * values, -1, keepdims=True)
    return delta * inverse - share * values * (along * inverse * inverse * inverse)


def kernel(
    sizes,
    x_ref,
    joined_ref,
    out_weight_ref,
    scale_ref,
    merge_ref,
    first_ref,
    second_ref,
    unfold_ref,
    g_ref,
    output_ref,
    grad_ref,
    xe,
    me,
    de,
    le,
    wm,
    wf,
    ws,
    wu,
    stacked_ref,
    probs_ref,
    attn_back,
    send_a,
    recv_a,
    merged_all,
    columns_all,
    send_o,
    recv_o,
    out_all,
    send_e,
    recv_e,
    delta_e,
    send_d,
    recv_d,
    delta_all,
    send_n,
    recv_n,
    send_c,
    columns_delta,
    send_m,
    recv_m,
    hidden_all,
    send_l,
    recv_l,
    send_sem,
    recv_sem,
    local_sem,
):
    n_lat, n_lon, n_mp, nbi, nbj, cells = sizes
    width = x_ref.shape[-1]
    la, lo, p = lax.axis_index("lat"), lax.axis_index("lon"), lax.axis_index("mp")
    rows_q = 4 * nbi * cells
    coarse_q = nbi * cells
    nwi, nwj = nbi // 2, nbj // 2
    window = 4 * 4 * cells
    split = 2 if n_lat == 2 else 1

    def plus(dlat, dlon, dmp):
        return {
            "lat": lax.rem(la + dlat + n_lat, n_lat),
            "lon": lax.rem(lo + dlon + n_lon, n_lon),
            "mp": lax.rem(p + dmp + n_mp, n_mp),
        }

    partners = set()
    for dlat, dlon in ((1, 0), (0, 1), (1, 1)):
        for sign in (1, -1):
            partners.add((sign * dlat % n_lat, sign * dlon % n_lon, 0))
    for by in range(1, n_lon):
        partners.add((0, by, 0))
    for by in range(1, n_mp):
        partners.add((0, 0, by))
    partners = sorted(partners)
    barrier = pltpu.get_barrier_semaphore()
    for offset in partners:
        pl.semaphore_signal(
            barrier, inc=1, device_id=plus(*offset), device_id_type=pl.DeviceIdType.MESH
        )
    pl.semaphore_wait(barrier, len(partners))

    count = [0]
    sent = []

    def send(src, dst, device):
        i = count[0]
        count[0] += 1
        copy = pltpu.make_async_remote_copy(
            src_ref=src,
            dst_ref=dst,
            send_sem=send_sem.at[i],
            recv_sem=recv_sem.at[i],
            device_id=device,
            device_id_type=pl.DeviceIdType.MESH,
        )
        copy.start()
        sent.append(copy)
        return copy

    def arrive(copies):
        for copy in copies:
            copy.wait_recv()

    def to_peers(src_of, dst):
        copies = []
        for by in range(1, n_mp):
            device = plus(0, 0, by)
            copies.append(send(src_of(device["mp"]), dst.at[p], device))
        return copies

    def sum_peers(own, dst):
        total = own.astype(f32)
        for by in range(1, n_mp):
            total = total + dst[lax.rem(p + by, n_mp)].astype(f32)
        return total

    halo = [
        send(x_ref.at[pl.ds(1, nbj - 1), :, 0], xe.at[pl.ds(1, nbj - 1), :, nbi], plus(-1, 0, 0)),
        send(x_ref.at[0, :, pl.ds(1, nbi - 1)], xe.at[nbj, :, pl.ds(1, nbi - 1)], plus(0, -1, 0)),
        send(x_ref.at[0, :, 0], xe.at[nbj, :, nbi], plus(-1, -1, 0)),
    ]
    gradient_moves = to_peers(lambda q: g_ref.at[q], delta_e)

    owned = ((merge_ref, wm), (first_ref, wf), (second_ref, ws), (unfold_ref, wu))
    own_copies = []
    for i, (src, dst) in enumerate(owned):
        copy = pltpu.make_async_copy(src, dst.at[lo], local_sem.at[i])
        copy.start()
        own_copies.append(copy)
    jobs = []
    for src, dst, pieces in (
        (merge_ref, wm, 1),
        (first_ref, wf, 2),
        (unfold_ref, wu, 1),
        (second_ref, ws, 2),
    ):
        rows = src.shape[0] // pieces
        for k in range(pieces):
            jobs.append((src, dst, k * rows, rows // split))
    relay = n_lon == 4
    started = {}
    across = {}

    def guarded(condition, action):
        if condition is None:
            action()
        else:
            pl.when(condition)(action)

    def remote(src, dst, device, i, j):
        return pltpu.make_async_remote_copy(
            src_ref=src,
            dst_ref=dst,
            send_sem=send_sem.at[i],
            recv_sem=recv_sem.at[j],
            device_id=device,
            device_id_type=pl.DeviceIdType.MESH,
        )

    guarded_sends = []

    def begin(i):
        src, dst, base, part = jobs[i]
        mine = pl.ds(pl.multiple_of(base + la * part, part) if split > 1 else base, part)
        first_index = count[0]
        count[0] += n_lon
        moves = {}
        for by in range(1, n_lon):
            index = first_index + by
            copy = remote(src.at[mine], dst.at[lo, mine], plus(0, by, 0), index, index)
            condition = None
            if relay and by == 1:
                condition = lo != n_lon - 1
            if relay and by == n_lon - 1:
                condition = lo != 0
            guarded(condition, copy.start)
            guarded_sends.append((condition, copy))
            moves[by] = copy
        started[i] = (moves, mine, first_index)

    def pass_on(i):
        dst = jobs[i][1]
        moves, mine, first_index = started[i]
        across[i] = []
        for by in [2, 1, 3] if relay else range(1, n_lon):
            owner = lax.rem(lo - by + n_lon, n_lon)
            moves[by].wait_recv()
            held = dst.at[owner, mine]
            if relay and by == 2:
                up = remote(held, held, plus(0, 1, 0), first_index, first_index + 3)
                down = remote(held, held, plus(0, -1, 0), first_index, first_index + 1)
                for condition, copy in ((lo == 2, up), (lo == 1, down)):
                    guarded(condition, copy.start)
                    guarded_sends.append((condition, copy))
            if split > 1:
                across[i].append(send(held, held, plus(1, 0, 0)))

    def ready(which, numbers):
        for i in numbers:
            arrive(across[i])
        own_copies[which].wait()

    for i in (0, 1, 2):
        begin(i)

    xe[pl.ds(0, nbj), :, pl.ds(0, nbi)] = x_ref[...]
    arrive(halo)

    def window_blocks(ref):
        parts = []
        for wi in range(nwi):
            for wj in range(nwj):
                for u in range(2):
                    for v in range(2):
                        block = ref[2 * wj + v + 1, :, 2 * wi + u + 1].astype(f32)
                        parts.append(block.reshape(4 * cells, ref.shape[-1]))
        return jnp.concatenate(parts, 0)

    def block_at(index):
        rest, v = divmod(index, 2)
        rest, u = divmod(rest, 2)
        wi, wj = divmod(rest, nwj)
        return 2 * wj + v + 1, 2 * wi + u + 1

    source = window_blocks(xe)
    normed = norm_parts(source, -1)[0].astype(bf16)
    joined = joined_ref[...]
    stacked = dot(normed, joined).astype(bf16)
    stacked_ref[...] = stacked
    local = joined.shape[1] // 3
    heads = scale_ref.shape[0] // n_mp
    head = local // heads
    t_half = lax.broadcasted_iota(jnp.int32, (window, window), 0) // (window // 2)
    s_half = lax.broadcasted_iota(jnp.int32, (window, window), 1) // (window // 2)
    last = (la == n_lat - 1).astype(f32)
    same = (t_half == s_half).astype(f32)
    gate = jnp.maximum(same, 1.0 - last)

    def slices(w, h):
        def part(k):
            at = k * local + h * head
            return stacked_ref[pl.ds(w * window, window), at : at + head].astype(f32)

        return part(0), part(1), part(2)

    mixed_windows = []
    for w in range(nwi * nwj):
        per_head = []
        for h in range(heads):
            query, key, value = slices(w, h)
            scale = scale_ref[p * heads + h]
            scores = scale * dot(unit(query).astype(bf16), unit(key).astype(bf16), 1, 1)
            raw = jnp.exp(scores)
            if w // nwj == nwi - 1:
                raw = raw * gate
            prob = raw / jnp.sum(raw, -1, keepdims=True)
            probs_ref[w * heads + h] = prob
            per_head.append(dot(prob.astype(bf16), value.astype(bf16)))
        mixed_windows.append(jnp.concatenate(per_head, 1))
    mixed = jnp.concatenate(mixed_windows, 0)
    block_rows = 4 * cells
    for index in range(nbi * nbj):
        bj, bi = block_at(index)
        block = mixed[index * block_rows : (index + 1) * block_rows]
        me[bj, :, bi] = block.reshape(4, cells, local).astype(bf16)
    back = [
        send(me.at[pl.ds(1, nbj - 1), :, nbi], me.at[pl.ds(1, nbj - 1), :, 0], plus(1, 0, 0)),
        send(me.at[nbj, :, pl.ds(1, nbi - 1)], me.at[0, :, pl.ds(1, nbi - 1)], plus(0, 1, 0)),
        send(me.at[nbj, :, nbi], me.at[0, :, 0], plus(1, 1, 0)),
    ]
    pass_on(0)
    for i in (3, 4, 5):
        begin(i)
    arrive(back)
    mixed_back = me[pl.ds(0, nbj), :, pl.ds(0, nbi)].astype(f32).reshape(n_mp * rows_q, local)
    partial = dot(mixed_back.astype(bf16), out_weight_ref[...]).astype(bf16)
    send_a[...] = partial.reshape(n_mp, rows_q, width)
    moves = to_peers(lambda q: send_a.at[q], recv_a)
    arrive(moves)
    own_fine = x_ref[p].astype(f32).reshape(rows_q, width)
    hidden = (own_fine + sum_peers(send_a[p], recv_a)).astype(bf16)
    hidden = hidden.astype(f32).reshape(4, coarse_q, width)
    merge_normal, merge_scale = norm_parts(hidden, (0, 2))
    merged_all[p] = merge_normal.astype(bf16)
    moves = to_peers(lambda q: merged_all.at[p], merged_all)
    pass_on(1)
    ready(0, (0,))
    merge_full = wm[...].reshape(4 * width, wm.shape[-1])
    arrive(moves)
    columns = jnp.zeros((n_mp * coarse_q, wm.shape[-1]), f32)
    for s in range(4):
        tokens = merged_all[:, s].reshape(n_mp * coarse_q, width)
        columns = columns + dot(tokens, merge_full[s * width : (s + 1) * width])
    columns_all[p] = columns.astype(bf16)
    moves = to_peers(lambda q: columns_all.at[p], columns_all)
    pass_on(2)

    for q in range(n_mp):
        @pl.when(p == q)
        def _(q=q):
            delta_e[q] = g_ref[q]

    arrive(gradient_moves)
    pass_on(3)
    ready(3, (3,))
    tokens_delta = delta_e[...].reshape(n_mp * coarse_q, width)
    unfold_full = wu[...].reshape(n_lon * wu.shape[1], width)
    coarse_width = unfold_full.shape[0]
    term = dot(tokens_delta, unfold_full, 1, 1).astype(bf16)
    send_d[...] = term.reshape(n_mp, coarse_q, coarse_width)
    moves_d = to_peers(lambda q: send_d.at[q], recv_d)

    arrive(moves)
    coarse = jnp.concatenate([columns_all[r] for r in range(n_mp)], 1).astype(f32)
    coarse_norm = norm_parts(coarse, -1)[0].astype(bf16)
    ready(1, (1, 2))
    first_full = wf[...].reshape(coarse_width, wf.shape[-1])
    inner = dot(coarse_norm, first_full).astype(bf16).astype(f32)
    activated = gelu(inner).astype(bf16)
    pass_on(4)
    arrive(moves_d)
    delta_own = sum_peers(send_d[p], recv_d).astype(bf16)
    delta_all[p] = delta_own
    moves_d = to_peers(lambda q: delta_all.at[p], delta_all)
    pass_on(5)
    ready(2, (4, 5))
    outer = jnp.concatenate([dot(activated, ws[k]) for k in range(n_lon)], 1).astype(bf16)
    send_o[...] = outer.reshape(n_mp, coarse_q, coarse_width)
    moves_o = to_peers(lambda q: send_o.at[q], recv_o)

    arrive(moves_o)
    own_coarse = jnp.concatenate(
        [columns_all[r, pl.ds(pl.multiple_of(p * coarse_q, coarse_q), coarse_q)] for r in range(n_mp)], 1
    ).astype(f32)
    out_all[p] = (own_coarse + sum_peers(send_o[p], recv_o)).astype(bf16)
    moves_o = to_peers(lambda q: out_all.at[p], out_all)

    arrive(moves_d)
    delta_coarse_out = delta_all[...].reshape(n_mp * coarse_q, coarse_width)
    second_width = ws.shape[-1]
    delta_active = jnp.zeros((n_mp * coarse_q, ws.shape[1]), f32)
    for k in range(n_lon):
        piece = delta_coarse_out[:, k * second_width : (k + 1) * second_width]
        delta_active = delta_active + dot(piece, ws[k], 1, 1)
    delta_inner = (delta_active.astype(bf16).astype(f32) * gelu_back(inner)).astype(bf16)
    term = dot(delta_inner, first_full, 1, 1).astype(bf16)
    send_n[...] = term.reshape(n_mp, coarse_q, coarse_width)
    moves_n = to_peers(lambda q: send_n.at[q], recv_n)

    arrive(moves_o)
    coarse_out = out_all[...].reshape(n_mp * coarse_q, coarse_width)
    send_e[...] = dot(coarse_out, unfold_full).astype(bf16).reshape(n_mp, coarse_q, width)
    moves_e = to_peers(lambda q: send_e.at[q], recv_e)

    arrive(moves_n)
    delta_norm = sum_peers(send_n[p], recv_n).astype(bf16).astype(f32)
    own_normal, own_scale = norm_parts(own_coarse, -1)
    pulled = norm_back(delta_norm, own_normal, own_scale, -1).astype(bf16).astype(f32)
    delta_coarse = (delta_own.astype(f32) + pulled).astype(bf16)
    stripe = wm.shape[-1]
    for r in range(n_mp):
        send_c[r] = delta_coarse[:, r * stripe : (r + 1) * stripe]
    moves_c = to_peers(lambda q: send_c.at[q], columns_delta)
    columns_delta[p] = send_c[p]

    arrive(moves_e)
    recv_e[p] = send_e[p]
    output_ref[...] = (hidden + recv_e[...].astype(f32)).astype(bf16)

    arrive(moves_c)
    delta_columns = columns_delta[...].reshape(n_mp * coarse_q, stripe)
    for s in range(4):
        piece = dot(delta_columns, merge_full[s * width : (s + 1) * width], 1, 1).astype(bf16)
        send_m[:, s] = piece.reshape(n_mp, coarse_q, width)
    moves = to_peers(lambda q: send_m.at[q], recv_m)
    arrive(moves)
    delta_merged = sum_peers(send_m[p], recv_m).astype(bf16).astype(f32)
    pulled = norm_back(delta_merged, merge_normal, merge_scale, (0, 2)).astype(bf16).astype(f32)
    delta_hidden = (g_ref[...].astype(f32) + pulled).astype(bf16)
    hidden_all[p] = delta_hidden
    moves = to_peers(lambda q: hidden_all.at[p], hidden_all)
    arrive(moves)

    delta_back = dot(
        hidden_all[...].reshape(n_mp * rows_q, width), out_weight_ref[...], 1, 1
    ).astype(bf16).astype(f32)
    de[pl.ds(0, nbj), :, pl.ds(0, nbi)] = delta_back.reshape(nbj, 4, nbi, cells, local).astype(bf16)
    halo = [
        send(de.at[pl.ds(1, nbj - 1), :, 0], de.at[pl.ds(1, nbj - 1), :, nbi], plus(-1, 0, 0)),
        send(de.at[0, :, pl.ds(1, nbi - 1)], de.at[nbj, :, pl.ds(1, nbi - 1)], plus(0, -1, 0)),
        send(de.at[0, :, 0], de.at[nbj, :, nbi], plus(-1, -1, 0)),
    ]
    arrive(halo)
    delta_mixed = window_blocks(de).astype(bf16)
    for w in range(nwi * nwj):
        grads = [[], [], []]
        for h in range(heads):
            query, key, value = slices(w, h)
            scale = scale_ref[p * heads + h]
            prob = probs_ref[w * heads + h]
            delta = delta_mixed[w * window : (w + 1) * window, h * head : (h + 1) * head]
            delta_prob = dot(delta, value.astype(bf16), 1, 1).astype(bf16).astype(f32)
            delta_value = dot(prob.astype(bf16), delta, 0, 0)
            inside = jnp.sum(delta_prob * prob, -1, keepdims=True)
            delta_score = (scale * (prob * (delta_prob - inside))).astype(bf16)
            delta_query = dot(delta_score, unit(key).astype(bf16)).astype(bf16).astype(f32)
            delta_key = dot(delta_score, unit(query).astype(bf16), 0, 0).astype(bf16).astype(f32)
            grads[0].append(unit_back(delta_query, query))
            grads[1].append(unit_back(delta_key, key))
            grads[2].append(delta_value)
        attn_back[pl.ds(w * window, window), :] = jnp.concatenate(
            grads[0] + grads[1] + grads[2], 1
        ).astype(bf16)
    delta_normed = dot(attn_back[...], joined_ref[...], 1, 1)
    for index in range(nbi * nbj):
        bj, bi = block_at(index)
        block = delta_normed[index * block_rows : (index + 1) * block_rows]
        send_l[bj % n_mp, :, bi - 1] = block.reshape(4, cells, width).astype(bf16)
    moves = to_peers(lambda q: send_l.at[q], recv_l)
    column = jnp.where(p == 0, n_mp, p)
    own_source = xe[column, :, pl.ds(1, nbi)].astype(f32)
    source_normal, source_scale = norm_parts(own_source, -1)
    arrive(moves)
    delta_source = sum_peers(send_l[p], recv_l).astype(bf16).astype(f32)
    delta_source = norm_back(delta_source, source_normal, source_scale, -1)
    le[:, pl.ds(1, nbi)] = delta_source.astype(bf16)

    final = count[0]
    count[0] += 2

    def last_copy(i, src, dst, device):
        return pltpu.make_async_remote_copy(
            src_ref=src,
            dst_ref=dst,
            send_sem=send_sem.at[final + i],
            recv_sem=recv_sem.at[final + i],
            device_id=device,
            device_id_type=pl.DeviceIdType.MESH,
        )

    first_column = (p == 0).astype(jnp.int32)
    corner = last_copy(0, le.at[:, nbi], le.at[:, 0], plus(1, first_column, 0))
    corner.start()
    rest = last_copy(1, le.at[:, pl.ds(1, nbi - 1)], recv_l.at[p, :, pl.ds(1, nbi - 1)], plus(0, 1, 0))

    @pl.when(p == 0)
    def _():
        rest.start()
        rest.wait()

    @pl.when(p != 0)
    def _():
        recv_l[p, :, pl.ds(1, nbi - 1)] = le[:, pl.ds(1, nbi - 1)]

    corner.wait()
    recv_l[p, :, 0] = le[:, 0]
    own_delta = recv_l[p].astype(f32).reshape(4, coarse_q, width)
    grad_ref[...] = (delta_hidden.astype(f32) + own_delta).astype(bf16)
    for copy in sent:
        copy.wait_send()
    for condition, copy in guarded_sends:
        guarded(condition, copy.wait_send)


def per_device(
    sharp_resolution_vectors,
    queries_keys_weights,
    values_weights,
    attn_result_weights,
    score_factors_by_lane,
    tile_merging_weights,
    shrunk_dense_first,
    shrunk_dense_second,
    tile_unfolding_weights,
    result_gradient,
):
    levels, row_count, column_count, width = sharp_resolution_vectors.shape
    n_lat, n_lon, n_mp = (lax.axis_size(name) for name in ("lat", "lon", "mp"))
    nbi, nbj = row_count // HALF, column_count // HALF
    cells = levels * (HALF // 2) ** 2
    assert nbj == n_mp and tile_unfolding_weights.shape[1] == width

    def to_blocks(value):
        columns = value.shape[2] // HALF
        value = value.reshape(levels, nbi, HALF // 2, 2, columns, HALF // 2, 2, width)
        value = value.transpose(4, 3, 6, 1, 0, 2, 5, 7)
        return value.reshape(columns, 4, nbi, cells, width)

    def from_blocks(value):
        value = value.reshape(2, 2, nbi, levels, HALF // 2, HALF // 2, width)
        value = value.transpose(3, 2, 4, 0, 5, 1, 6)
        return value.reshape(levels, row_count, HALF, width)

    blocks = to_blocks(sharp_resolution_vectors)
    local = values_weights.shape[1]
    joined = jnp.concatenate([queries_keys_weights.reshape(width, 2 * local), values_weights], 1)
    coarse_q = nbi * cells
    rows_q = 4 * coarse_q
    gradient = to_blocks(result_gradient).reshape(4, coarse_q, width)
    weights = (tile_merging_weights, shrunk_dense_first, shrunk_dense_second, tile_unfolding_weights)
    coarse_width = n_lon * tile_unfolding_weights.shape[0]
    stripe = tile_merging_weights.shape[1]
    heads = score_factors_by_lane.shape[0] // n_mp
    window = 16 * cells
    windows = (nbi // 2) * (nbj // 2)
    vm = pltpu.VMEM
    fine = (n_mp, rows_q, width)
    coarse = (n_mp, coarse_q, coarse_width)
    quarter = (n_mp, coarse_q, width)
    grouped = (n_mp, 4, coarse_q, width)
    pieces = (n_mp, 4, nbi, cells, width)
    scratch = [
        vm((nbj + 1, 4, nbi + 1, cells, width), bf16),
        vm((nbj + 1, 4, nbi + 1, cells, local), bf16),
        vm((nbj + 1, 4, nbi + 1, cells, local), bf16),
        vm((4, nbi + 1, cells, width), bf16),
        *[vm((n_lon,) + w.shape, bf16) for w in weights],
        vm((windows * window, 3 * local), bf16),
        vm((windows * heads, window, window), f32),
        vm((windows * window, 3 * local), bf16),
        vm(fine, bf16),
        vm(fine, bf16),
        vm(grouped, bf16),
        vm((n_mp, n_mp * coarse_q, stripe), bf16),
        vm(coarse, bf16),
        vm(coarse, bf16),
        vm(coarse, bf16),
        vm(quarter, bf16),
        vm(quarter, bf16),
        vm(quarter, bf16),
        vm(coarse, bf16),
        vm(coarse, bf16),
        vm(coarse, bf16),
        vm(coarse, bf16),
        vm(coarse, bf16),
        vm((n_mp, coarse_q, stripe), bf16),
        vm((n_mp, coarse_q, stripe), bf16),
        vm(grouped, bf16),
        vm(grouped, bf16),
        vm(grouped, bf16),
        vm(pieces, bf16),
        vm(pieces, bf16),
    ]
    copies = 11 + 14 * (n_mp - 1) + 12 * n_lon
    scratch += [
        pltpu.SemaphoreType.DMA((copies,)),
        pltpu.SemaphoreType.DMA((copies,)),
        pltpu.SemaphoreType.DMA((4,)),
    ]
    inside = pl.BlockSpec(memory_space=pltpu.VMEM)
    outside = pl.BlockSpec(memory_space=pl.ANY)
    shape = jax.ShapeDtypeStruct((4, coarse_q, width), bf16)
    output, grad = pl.pallas_call(
        functools.partial(kernel, (n_lat, n_lon, n_mp, nbi, nbj, cells)),
        out_shape=(shape, shape),
        in_specs=[inside] * 3
        + [pl.BlockSpec(memory_space=pltpu.SMEM)]
        + [outside] * 4
        + [inside],
        out_specs=(inside, inside),
        scratch_shapes=scratch,
        compiler_params=pltpu.CompilerParams(
            collective_id=0, has_side_effects=True, vmem_limit_bytes=56 * 2**20
        ),
        name="unet_step",
    )(blocks, joined, attn_result_weights, score_factors_by_lane, *weights, gradient)
    return (from_blocks(output), from_blocks(grad))


def solution(mesh):
    in_specs = (
        P(None, "lat", "lon", None),
        P(None, None, "mp"),
        P(None, "mp"),
        P("mp", None),
        P(),
        P("lon", "mp"),
        P("lon", "mp"),
        P("mp", "lon"),
        P("lon", "mp"),
        P(None, "lat", ("lon", "mp"), None),
    )
    out_specs = (P(None, "lat", ("lon", "mp"), None), P(None, "lat", ("lon", "mp"), None))
    return jax.shard_map(
        per_device, mesh=mesh, in_specs=in_specs, out_specs=out_specs, check_vma=False
    )
```

```python
import functools
import jax
import jax.numpy as jnp
from jax import lax
from jax.experimental import pallas as pl
from jax.experimental.pallas import tpu as pltpu
from jax.sharding import PartitionSpec as P

TILE_SIDE_CELLS = 8
HALF = TILE_SIDE_CELLS // 2

epsilon = 1e-05
bf16 = jnp.bfloat16
f32 = jnp.float32


def dot(a, b, ca=1, cb=0):
    return lax.dot_general(a, b, (((ca,), (cb,)), ((), ())), preferred_element_type=f32)


def norm_parts(values, axes):
    center = values - jnp.mean(values, axes, keepdims=True)
    spread = jnp.mean(center * center, axes, keepdims=True)
    scale = lax.rsqrt(spread + epsilon)
    return center * scale, scale


def norm_back(delta, normal, scale, axes):
    return scale * (
        delta
        - jnp.mean(delta, axes, keepdims=True)
        - normal * jnp.mean(delta * normal, axes, keepdims=True)
    )


GELU_A = 0.7978845608028654
GELU_B = 0.044715


def gelu(x):
    return 0.5 * x * (1.0 + jnp.tanh(GELU_A * (x + GELU_B * x * x * x)))


def gelu_back(x):
    t = jnp.tanh(GELU_A * (x + GELU_B * x * x * x))
    return 0.5 * (1.0 + t) + 0.5 * x * (1.0 - t * t) * GELU_A * (1.0 + 3.0 * GELU_B * x * x)


def unit(values):
    length = jnp.sqrt(jnp.sum(values * values, -1, keepdims=True))
    return values / jnp.maximum(length, 1.0)


def unit_back(delta, values):
    length = jnp.sqrt(jnp.sum(values * values, -1, keepdims=True))
    inverse = 1.0 / jnp.maximum(length, 1.0)
    share = jnp.where(length > 1.0, 1.0, jnp.where(length == 1.0, 0.5, 0.0))
    along = jnp.sum(delta * values, -1, keepdims=True)
    return delta * inverse - share * values * (along * inverse * inverse * inverse)


def kernel(
    sizes,
    x_ref,
    joined_ref,
    out_weight_ref,
    scale_ref,
    merge_ref,
    first_ref,
    second_ref,
    unfold_ref,
    g_ref,
    output_ref,
    grad_ref,
    xe,
    me,
    de,
    le,
    wm,
    wf,
    ws,
    wu,
    stacked_ref,
    probs_ref,
    attn_back,
    send_a,
    recv_a,
    merged_all,
    columns_all,
    send_o,
    recv_o,
    out_all,
    send_e,
    recv_e,
    delta_e,
    send_d,
    recv_d,
    delta_all,
    send_n,
    recv_n,
    send_c,
    columns_delta,
    send_m,
    recv_m,
    hidden_all,
    send_l,
    recv_l,
    send_sem,
    recv_sem,
    local_sem,
):
    n_lat, n_lon, n_mp, nbi, nbj, cells = sizes
    width = x_ref.shape[-1]
    la, lo, p = lax.axis_index("lat"), lax.axis_index("lon"), lax.axis_index("mp")
    rows_q = 4 * nbi * cells
    coarse_q = nbi * cells
    nwi, nwj = nbi // 2, nbj // 2
    window = 4 * 4 * cells
    split = 2 if n_lat == 2 else 1

    def plus(dlat, dlon, dmp):
        return {
            "lat": lax.rem(la + dlat + n_lat, n_lat),
            "lon": lax.rem(lo + dlon + n_lon, n_lon),
            "mp": lax.rem(p + dmp + n_mp, n_mp),
        }

    partners = set()
    for dlat, dlon in ((1, 0), (0, 1), (1, 1)):
        for sign in (1, -1):
            partners.add((sign * dlat % n_lat, sign * dlon % n_lon, 0))
    for by in range(1, n_lon):
        partners.add((0, by, 0))
    for by in range(1, n_mp):
        partners.add((0, 0, by))
    partners = sorted(partners)
    barrier = pltpu.get_barrier_semaphore()
    for offset in partners:
        pl.semaphore_signal(
            barrier, inc=1, device_id=plus(*offset), device_id_type=pl.DeviceIdType.MESH
        )
    pl.semaphore_wait(barrier, len(partners))

    count = [0]
    sent = []

    def send(src, dst, device):
        i = count[0]
        count[0] += 1
        copy = pltpu.make_async_remote_copy(
            src_ref=src,
            dst_ref=dst,
            send_sem=send_sem.at[i],
            recv_sem=recv_sem.at[i],
            device_id=device,
            device_id_type=pl.DeviceIdType.MESH,
        )
        copy.start()
        sent.append(copy)
        return copy

    def arrive(copies):
        for copy in copies:
            copy.wait_recv()

    def to_peers(src_of, dst):
        copies = []
        for by in range(1, n_mp):
            device = plus(0, 0, by)
            copies.append(send(src_of(device["mp"]), dst.at[p], device))
        return copies

    def sum_peers(own, dst):
        total = own.astype(f32)
        for by in range(1, n_mp):
            total = total + dst[lax.rem(p + by, n_mp)].astype(f32)
        return total

    halo = [
        send(x_ref.at[pl.ds(1, nbj - 1), :, 0], xe.at[pl.ds(1, nbj - 1), :, nbi], plus(-1, 0, 0)),
        send(x_ref.at[0, :, pl.ds(1, nbi - 1)], xe.at[nbj, :, pl.ds(1, nbi - 1)], plus(0, -1, 0)),
        send(x_ref.at[0, :, 0], xe.at[nbj, :, nbi], plus(-1, -1, 0)),
    ]
    gradient_moves = to_peers(lambda q: g_ref.at[q], delta_e)

    owned = ((merge_ref, wm), (first_ref, wf), (second_ref, ws), (unfold_ref, wu))
    own_copies = []
    for i, (src, dst) in enumerate(owned):
        copy = pltpu.make_async_copy(src, dst.at[lo], local_sem.at[i])
        copy.start()
        own_copies.append(copy)
    jobs = []
    for src, dst, pieces in (
        (merge_ref, wm, 1),
        (first_ref, wf, 2),
        (unfold_ref, wu, 1),
        (second_ref, ws, 2),
    ):
        rows = src.shape[0] // pieces
        for k in range(pieces):
            jobs.append((src, dst, k * rows, rows // split))
    relay = n_lon == 4
    started = {}
    across = {}

    def guarded(condition, action):
        if condition is None:
            action()
        else:
            pl.when(condition)(action)

    def remote(src, dst, device, i, j):
        return pltpu.make_async_remote_copy(
            src_ref=src,
            dst_ref=dst,
            send_sem=send_sem.at[i],
            recv_sem=recv_sem.at[j],
            device_id=device,
            device_id_type=pl.DeviceIdType.MESH,
        )

    guarded_sends = []

    def begin(i):
        src, dst, base, part = jobs[i]
        mine = pl.ds(pl.multiple_of(base + la * part, part) if split > 1 else base, part)
        first_index = count[0]
        count[0] += n_lon
        moves = {}
        for by in range(1, n_lon):
            index = first_index + by
            copy = remote(src.at[mine], dst.at[lo, mine], plus(0, by, 0), index, index)
            condition = None
            if relay and by == 1:
                condition = lo != n_lon - 1
            if relay and by == n_lon - 1:
                condition = lo != 0
            guarded(condition, copy.start)
            guarded_sends.append((condition, copy))
            moves[by] = copy
        started[i] = (moves, mine, first_index)

    def pass_on(i):
        dst = jobs[i][1]
        moves, mine, first_index = started[i]
        across[i] = []
        for by in [2, 1, 3] if relay else range(1, n_lon):
            owner = lax.rem(lo - by + n_lon, n_lon)
            moves[by].wait_recv()
            held = dst.at[owner, mine]
            if relay and by == 2:
                up = remote(held, held, plus(0, 1, 0), first_index, first_index + 3)
                down = remote(held, held, plus(0, -1, 0), first_index, first_index + 1)
                for condition, copy in ((lo == 2, up), (lo == 1, down)):
                    guarded(condition, copy.start)
                    guarded_sends.append((condition, copy))
            if split > 1:
                across[i].append(send(held, held, plus(1, 0, 0)))

    def ready(which, numbers):
        for i in numbers:
            arrive(across[i])
        own_copies[which].wait()

    for i in (0, 1, 2):
        begin(i)

    xe[pl.ds(0, nbj), :, pl.ds(0, nbi)] = x_ref[...]
    arrive(halo)

    def window_blocks(ref):
        parts = []
        for wi in range(nwi):
            for wj in range(nwj):
                for u in range(2):
                    for v in range(2):
                        block = ref[2 * wj + v + 1, :, 2 * wi + u + 1].astype(f32)
                        parts.append(block.reshape(4 * cells, ref.shape[-1]))
        return jnp.concatenate(parts, 0)

    def block_at(index):
        rest, v = divmod(index, 2)
        rest, u = divmod(rest, 2)
        wi, wj = divmod(rest, nwj)
        return 2 * wj + v + 1, 2 * wi + u + 1

    source = window_blocks(xe)
    normed = norm_parts(source, -1)[0].astype(bf16)
    joined = joined_ref[...]
    stacked = dot(normed, joined).astype(bf16)
    stacked_ref[...] = stacked
    local = joined.shape[1] // 3
    heads = scale_ref.shape[0] // n_mp
    head = local // heads
    t_half = lax.broadcasted_iota(jnp.int32, (window, window), 0) // (window // 2)
    s_half = lax.broadcasted_iota(jnp.int32, (window, window), 1) // (window // 2)
    last = (la == n_lat - 1).astype(f32)
    same = (t_half == s_half).astype(f32)
    gate = jnp.maximum(same, 1.0 - last)

    def slices(w, h):
        def part(k):
            at = k * local + h * head
            return stacked_ref[pl.ds(w * window, window), at : at + head].astype(f32)

        return part(0), part(1), part(2)

    pass_on(0)
    mixed_windows = []
    for w in range(nwi * nwj):
        per_head = []
        for h in range(heads):
            query, key, value = slices(w, h)
            scale = scale_ref[p * heads + h]
            scores = scale * dot(unit(query).astype(bf16), unit(key).astype(bf16), 1, 1)
            raw = jnp.exp(scores)
            if w // nwj == nwi - 1:
                raw = raw * gate
            prob = raw / jnp.sum(raw, -1, keepdims=True)
            probs_ref[w * heads + h] = prob
            per_head.append(dot(prob.astype(bf16), value.astype(bf16)))
        mixed_windows.append(jnp.concatenate(per_head, 1))
    mixed = jnp.concatenate(mixed_windows, 0)
    block_rows = 4 * cells
    for index in range(nbi * nbj):
        bj, bi = block_at(index)
        block = mixed[index * block_rows : (index + 1) * block_rows]
        me[bj, :, bi] = block.reshape(4, cells, local).astype(bf16)
    back = [
        send(me.at[pl.ds(1, nbj - 1), :, nbi], me.at[pl.ds(1, nbj - 1), :, 0], plus(1, 0, 0)),
        send(me.at[nbj, :, pl.ds(1, nbi - 1)], me.at[0, :, pl.ds(1, nbi - 1)], plus(0, 1, 0)),
        send(me.at[nbj, :, nbi], me.at[0, :, 0], plus(1, 1, 0)),
    ]
    pass_on(1)
    for i in (3, 4, 5):
        begin(i)
    arrive(back)
    mixed_back = me[pl.ds(0, nbj), :, pl.ds(0, nbi)].astype(f32).reshape(n_mp * rows_q, local)
    partial = dot(mixed_back.astype(bf16), out_weight_ref[...]).astype(bf16)
    send_a[...] = partial.reshape(n_mp, rows_q, width)
    moves = to_peers(lambda q: send_a.at[q], recv_a)
    arrive(moves)
    own_fine = x_ref[p].astype(f32).reshape(rows_q, width)
    hidden = (own_fine + sum_peers(send_a[p], recv_a)).astype(bf16)
    hidden = hidden.astype(f32).reshape(4, coarse_q, width)
    merge_normal, merge_scale = norm_parts(hidden, (0, 2))
    merged_all[p] = merge_normal.astype(bf16)
    moves = to_peers(lambda q: merged_all.at[p], merged_all)
    pass_on(2)
    ready(0, (0,))
    merge_full = wm[...].reshape(4 * width, wm.shape[-1])
    arrive(moves)
    columns = jnp.zeros((n_mp * coarse_q, wm.shape[-1]), f32)
    for s in range(4):
        tokens = merged_all[:, s].reshape(n_mp * coarse_q, width)
        columns = columns + dot(tokens, merge_full[s * width : (s + 1) * width])
    columns_all[p] = columns.astype(bf16)
    moves = to_peers(lambda q: columns_all.at[p], columns_all)
    pass_on(3)

    for q in range(n_mp):
        @pl.when(p == q)
        def _(q=q):
            delta_e[q] = g_ref[q]

    arrive(gradient_moves)
    ready(3, (3,))
    tokens_delta = delta_e[...].reshape(n_mp * coarse_q, width)
    unfold_full = wu[...].reshape(n_lon * wu.shape[1], width)
    coarse_width = unfold_full.shape[0]
    term = dot(tokens_delta, unfold_full, 1, 1).astype(bf16)
    send_d[...] = term.reshape(n_mp, coarse_q, coarse_width)
    moves_d = to_peers(lambda q: send_d.at[q], recv_d)

    arrive(moves)
    coarse = jnp.concatenate([columns_all[r] for r in range(n_mp)], 1).astype(f32)
    coarse_norm = norm_parts(coarse, -1)[0].astype(bf16)
    ready(1, (1, 2))
    first_full = wf[...].reshape(coarse_width, wf.shape[-1])
    inner = dot(coarse_norm, first_full).astype(bf16).astype(f32)
    activated = gelu(inner).astype(bf16)
    pass_on(4)
    arrive(moves_d)
    delta_own = sum_peers(send_d[p], recv_d).astype(bf16)
    delta_all[p] = delta_own
    moves_d = to_peers(lambda q: delta_all.at[p], delta_all)
    pass_on(5)
    ready(2, (4, 5))
    outer = jnp.concatenate([dot(activated, ws[k]) for k in range(n_lon)], 1).astype(bf16)
    send_o[...] = outer.reshape(n_mp, coarse_q, coarse_width)
    moves_o = to_peers(lambda q: send_o.at[q], recv_o)

    arrive(moves_o)
    own_coarse = jnp.concatenate(
        [columns_all[r, pl.ds(pl.multiple_of(p * coarse_q, coarse_q), coarse_q)] for r in range(n_mp)], 1
    ).astype(f32)
    out_all[p] = (own_coarse + sum_peers(send_o[p], recv_o)).astype(bf16)
    moves_o = to_peers(lambda q: out_all.at[p], out_all)

    arrive(moves_d)
    delta_coarse_out = delta_all[...].reshape(n_mp * coarse_q, coarse_width)
    second_width = ws.shape[-1]
    delta_active = jnp.zeros((n_mp * coarse_q, ws.shape[1]), f32)
    for k in range(n_lon):
        piece = delta_coarse_out[:, k * second_width : (k + 1) * second_width]
        delta_active = delta_active + dot(piece, ws[k], 1, 1)
    delta_inner = (delta_active.astype(bf16).astype(f32) * gelu_back(inner)).astype(bf16)
    term = dot(delta_inner, first_full, 1, 1).astype(bf16)
    send_n[...] = term.reshape(n_mp, coarse_q, coarse_width)
    moves_n = to_peers(lambda q: send_n.at[q], recv_n)

    arrive(moves_o)
    coarse_out = out_all[...].reshape(n_mp * coarse_q, coarse_width)
    send_e[...] = dot(coarse_out, unfold_full).astype(bf16).reshape(n_mp, coarse_q, width)
    moves_e = to_peers(lambda q: send_e.at[q], recv_e)

    arrive(moves_n)
    delta_norm = sum_peers(send_n[p], recv_n).astype(bf16).astype(f32)
    own_normal, own_scale = norm_parts(own_coarse, -1)
    pulled = norm_back(delta_norm, own_normal, own_scale, -1).astype(bf16).astype(f32)
    delta_coarse = (delta_own.astype(f32) + pulled).astype(bf16)
    stripe = wm.shape[-1]
    for r in range(n_mp):
        send_c[r] = delta_coarse[:, r * stripe : (r + 1) * stripe]
    moves_c = to_peers(lambda q: send_c.at[q], columns_delta)
    columns_delta[p] = send_c[p]

    arrive(moves_e)
    recv_e[p] = send_e[p]
    output_ref[...] = (hidden + recv_e[...].astype(f32)).astype(bf16)

    arrive(moves_c)
    delta_columns = columns_delta[...].reshape(n_mp * coarse_q, stripe)
    for s in range(4):
        piece = dot(delta_columns, merge_full[s * width : (s + 1) * width], 1, 1).astype(bf16)
        send_m[:, s] = piece.reshape(n_mp, coarse_q, width)
    moves = to_peers(lambda q: send_m.at[q], recv_m)
    arrive(moves)
    delta_merged = sum_peers(send_m[p], recv_m).astype(bf16).astype(f32)
    pulled = norm_back(delta_merged, merge_normal, merge_scale, (0, 2)).astype(bf16).astype(f32)
    delta_hidden = (g_ref[...].astype(f32) + pulled).astype(bf16)
    hidden_all[p] = delta_hidden
    moves = to_peers(lambda q: hidden_all.at[p], hidden_all)
    arrive(moves)

    delta_back = dot(
        hidden_all[...].reshape(n_mp * rows_q, width), out_weight_ref[...], 1, 1
    ).astype(bf16).astype(f32)
    de[pl.ds(0, nbj), :, pl.ds(0, nbi)] = delta_back.reshape(nbj, 4, nbi, cells, local).astype(bf16)
    halo = [
        send(de.at[pl.ds(1, nbj - 1), :, 0], de.at[pl.ds(1, nbj - 1), :, nbi], plus(-1, 0, 0)),
        send(de.at[0, :, pl.ds(1, nbi - 1)], de.at[nbj, :, pl.ds(1, nbi - 1)], plus(0, -1, 0)),
        send(de.at[0, :, 0], de.at[nbj, :, nbi], plus(-1, -1, 0)),
    ]
    arrive(halo)
    delta_mixed = window_blocks(de).astype(bf16)
    for w in range(nwi * nwj):
        grads = [[], [], []]
        for h in range(heads):
            query, key, value = slices(w, h)
            scale = scale_ref[p * heads + h]
            prob = probs_ref[w * heads + h]
            delta = delta_mixed[w * window : (w + 1) * window, h * head : (h + 1) * head]
            delta_prob = dot(delta, value.astype(bf16), 1, 1).astype(bf16).astype(f32)
            delta_value = dot(prob.astype(bf16), delta, 0, 0)
            inside = jnp.sum(delta_prob * prob, -1, keepdims=True)
            delta_score = (scale * (prob * (delta_prob - inside))).astype(bf16)
            delta_query = dot(delta_score, unit(key).astype(bf16)).astype(bf16).astype(f32)
            delta_key = dot(delta_score, unit(query).astype(bf16), 0, 0).astype(bf16).astype(f32)
            grads[0].append(unit_back(delta_query, query))
            grads[1].append(unit_back(delta_key, key))
            grads[2].append(delta_value)
        attn_back[pl.ds(w * window, window), :] = jnp.concatenate(
            grads[0] + grads[1] + grads[2], 1
        ).astype(bf16)
    delta_normed = dot(attn_back[...], joined_ref[...], 1, 1)
    for index in range(nbi * nbj):
        bj, bi = block_at(index)
        block = delta_normed[index * block_rows : (index + 1) * block_rows]
        send_l[bj % n_mp, :, bi - 1] = block.reshape(4, cells, width).astype(bf16)
    moves = to_peers(lambda q: send_l.at[q], recv_l)
    column = jnp.where(p == 0, n_mp, p)
    own_source = xe[column, :, pl.ds(1, nbi)].astype(f32)
    source_normal, source_scale = norm_parts(own_source, -1)
    arrive(moves)
    delta_source = sum_peers(send_l[p], recv_l).astype(bf16).astype(f32)
    delta_source = norm_back(delta_source, source_normal, source_scale, -1)
    le[:, pl.ds(1, nbi)] = delta_source.astype(bf16)

    final = count[0]
    count[0] += 2

    def last_copy(i, src, dst, device):
        return pltpu.make_async_remote_copy(
            src_ref=src,
            dst_ref=dst,
            send_sem=send_sem.at[final + i],
            recv_sem=recv_sem.at[final + i],
            device_id=device,
            device_id_type=pl.DeviceIdType.MESH,
        )

    first_column = (p == 0).astype(jnp.int32)
    corner = last_copy(0, le.at[:, nbi], le.at[:, 0], plus(1, first_column, 0))
    corner.start()
    rest = last_copy(1, le.at[:, pl.ds(1, nbi - 1)], recv_l.at[p, :, pl.ds(1, nbi - 1)], plus(0, 1, 0))

    @pl.when(p == 0)
    def _():
        rest.start()
        rest.wait()

    @pl.when(p != 0)
    def _():
        recv_l[p, :, pl.ds(1, nbi - 1)] = le[:, pl.ds(1, nbi - 1)]

    corner.wait()
    recv_l[p, :, 0] = le[:, 0]
    own_delta = recv_l[p].astype(f32).reshape(4, coarse_q, width)
    grad_ref[...] = (delta_hidden.astype(f32) + own_delta).astype(bf16)
    for copy in sent:
        copy.wait_send()
    for condition, copy in guarded_sends:
        guarded(condition, copy.wait_send)


def per_device(
    sharp_resolution_vectors,
    queries_keys_weights,
    values_weights,
    attn_result_weights,
    score_factors_by_lane,
    tile_merging_weights,
    shrunk_dense_first,
    shrunk_dense_second,
    tile_unfolding_weights,
    result_gradient,
):
    levels, row_count, column_count, width = sharp_resolution_vectors.shape
    n_lat, n_lon, n_mp = (lax.axis_size(name) for name in ("lat", "lon", "mp"))
    nbi, nbj = row_count // HALF, column_count // HALF
    cells = levels * (HALF // 2) ** 2
    assert nbj == n_mp and tile_unfolding_weights.shape[1] == width

    def to_blocks(value):
        columns = value.shape[2] // HALF
        value = value.reshape(levels, nbi, HALF // 2, 2, columns, HALF // 2, 2, width)
        value = value.transpose(4, 3, 6, 1, 0, 2, 5, 7)
        return value.reshape(columns, 4, nbi, cells, width)

    def from_blocks(value):
        value = value.reshape(2, 2, nbi, levels, HALF // 2, HALF // 2, width)
        value = value.transpose(3, 2, 4, 0, 5, 1, 6)
        return value.reshape(levels, row_count, HALF, width)

    blocks = to_blocks(sharp_resolution_vectors)
    local = values_weights.shape[1]
    joined = jnp.concatenate([queries_keys_weights.reshape(width, 2 * local), values_weights], 1)
    coarse_q = nbi * cells
    rows_q = 4 * coarse_q
    gradient = to_blocks(result_gradient).reshape(4, coarse_q, width)
    weights = (tile_merging_weights, shrunk_dense_first, shrunk_dense_second, tile_unfolding_weights)
    coarse_width = n_lon * tile_unfolding_weights.shape[0]
    stripe = tile_merging_weights.shape[1]
    heads = score_factors_by_lane.shape[0] // n_mp
    window = 16 * cells
    windows = (nbi // 2) * (nbj // 2)
    vm = pltpu.VMEM
    fine = (n_mp, rows_q, width)
    coarse = (n_mp, coarse_q, coarse_width)
    quarter = (n_mp, coarse_q, width)
    grouped = (n_mp, 4, coarse_q, width)
    pieces = (n_mp, 4, nbi, cells, width)
    scratch = [
        vm((nbj + 1, 4, nbi + 1, cells, width), bf16),
        vm((nbj + 1, 4, nbi + 1, cells, local), bf16),
        vm((nbj + 1, 4, nbi + 1, cells, local), bf16),
        vm((4, nbi + 1, cells, width), bf16),
        *[vm((n_lon,) + w.shape, bf16) for w in weights],
        vm((windows * window, 3 * local), bf16),
        vm((windows * heads, window, window), f32),
        vm((windows * window, 3 * local), bf16),
        vm(fine, bf16),
        vm(fine, bf16),
        vm(grouped, bf16),
        vm((n_mp, n_mp * coarse_q, stripe), bf16),
        vm(coarse, bf16),
        vm(coarse, bf16),
        vm(coarse, bf16),
        vm(quarter, bf16),
        vm(quarter, bf16),
        vm(quarter, bf16),
        vm(coarse, bf16),
        vm(coarse, bf16),
        vm(coarse, bf16),
        vm(coarse, bf16),
        vm(coarse, bf16),
        vm((n_mp, coarse_q, stripe), bf16),
        vm((n_mp, coarse_q, stripe), bf16),
        vm(grouped, bf16),
        vm(grouped, bf16),
        vm(grouped, bf16),
        vm(pieces, bf16),
        vm(pieces, bf16),
    ]
    copies = 11 + 14 * (n_mp - 1) + 12 * n_lon
    scratch += [
        pltpu.SemaphoreType.DMA((copies,)),
        pltpu.SemaphoreType.DMA((copies,)),
        pltpu.SemaphoreType.DMA((4,)),
    ]
    inside = pl.BlockSpec(memory_space=pltpu.VMEM)
    outside = pl.BlockSpec(memory_space=pl.ANY)
    shape = jax.ShapeDtypeStruct((4, coarse_q, width), bf16)
    output, grad = pl.pallas_call(
        functools.partial(kernel, (n_lat, n_lon, n_mp, nbi, nbj, cells)),
        out_shape=(shape, shape),
        in_specs=[inside] * 3
        + [pl.BlockSpec(memory_space=pltpu.SMEM)]
        + [outside] * 4
        + [inside],
        out_specs=(inside, inside),
        scratch_shapes=scratch,
        compiler_params=pltpu.CompilerParams(
            collective_id=0, has_side_effects=True, vmem_limit_bytes=56 * 2**20
        ),
        name="unet_step",
    )(blocks, joined, attn_result_weights, score_factors_by_lane, *weights, gradient)
    return (from_blocks(output), from_blocks(grad))


def solution(mesh):
    in_specs = (
        P(None, "lat", "lon", None),
        P(None, None, "mp"),
        P(None, "mp"),
        P("mp", None),
        P(),
        P("lon", "mp"),
        P("lon", "mp"),
        P("mp", "lon"),
        P("lon", "mp"),
        P(None, "lat", ("lon", "mp"), None),
    )
    out_specs = (P(None, "lat", ("lon", "mp"), None), P(None, "lat", ("lon", "mp"), None))
    return jax.shard_map(
        per_device, mesh=mesh, in_specs=in_specs, out_specs=out_specs, check_vma=False
    )
```
